32 devices in a mesh: grp: 2 (over y), tile: 4 (over x, core), tp: 4 (over z).
Axes of the slice: x: 2, y: 2, z: 4, core: 2. Of those that a mesh axis runs over, the one named last changes fastest.
Arguments:
- atmos_state: bfloat16 [4096, 1536], P(('grp', 'tile')), may hold values from -6 to 6
- atmos_gain: float32 [1536], replicated, may hold values from 0.25 to 1.75
- w_first: bfloat16 [1536, 3072], P(('grp', 'tile'), 'tp'), may hold values from -0.15625 to 0.15625
- w_second: bfloat16 [1536, 3072], P(('grp', 'tile'), 'tp'), may hold values from -0.109375 to 0.109375
- flux_proj: bfloat16 [1536, 256], replicated, may hold values from -0.15625 to 0.15625
- remap_index: int32 [64, 3], P(('grp', 'tile', 'tp')), may hold values from 0 to 3
- remap_weight: bfloat16 [64, 3, 128, 128], P(('grp', 'tile', 'tp')), may hold values from -0.3125 to 0.3125
- ocean_state: bfloat16 [64, 128, 256], P(('grp', 'tile'), 'tp'), may hold values from -6 to 6
- depth_levels: int32 [64, 128], P(('grp', 'tile'), 'tp'), may hold values from 0 to 16
- conv_kernel: float32 [3, 3, 256], replicated, may hold values from -2 to 2
- ocean_gain: float32 [256], replicated, may hold values from 0.25 to 1.75
- ocean_w_in: bfloat16 [256, 1024], replicated, may hold values from -0.375 to 0.375
- ocean_w_out: bfloat16 [1024, 256], replicated, may hold values from -0.1875 to 0.1875
- ocean_cotangent: bfloat16 [64, 128, 256], P(('grp', 'tile'), 'tp'), may hold values from -6 to 6
Outputs:
- atmos_out: bfloat16 [4096, 1536], P(('grp', 'tile', 'tp'))
- ocean_out: bfloat16 [64, 128, 256], P(('grp', 'tile'), 'tp')
- weight_grads: float32 [2048, 256], P(('grp', 'tile', 'tp'))
The draws below stay inside these ranges and needn't reach their ends.
Inputs may be any that keep to these rules, and one draw needn't show every extreme that they name: `remap_index`: index the 128-token blocks among the 512 atmosphere tokens of the same grp and tile indices as the ocean tile of that block. `depth_levels`: 0 marks land.
All inputs are finite; a program needn't handle non-finite values.
Results may differ from the reference program's by a relative error of at most 0.018.
Values may be sent and summed in bfloat16 or wider, within the bound.
No kernel may reach another device: no remote copies, remote signals or barrier semaphores. Data moves between devices by JAX's collectives and lax.ppermute only.
A program may use at most 64 MiB of HBM per device.

```python
import jax
import jax.numpy as jnp
from jax import lax

D = 1536
FF = 3072
C = 256
HID = 1024
LEV = 16
BLK = 128
KSRC = 3
TOK_DEV = 512
OX = 8
OY = 32
TOKENS = 4096
NXO = 64
NYO = 128
OBLK = 64
N_GRP = 2
N_TILE = 4
N_TP = 4


def plant(values, rng, least, top_value):
    shape = values.shape
    place = [jax.random.randint(jax.random.fold_in(rng, axis), (), 0, shape[axis]) for axis in range(len(shape))]
    values = values.at[tuple(place)].set(least)
    longest = shape.index(max(shape))
    place[longest] = (place[longest] + 1) % shape[longest]
    return values.at[tuple(place)].set(top_value)


def block_scale(key, dims, split, low, top_value):
    def one(dim, shards_of):
        steps = jax.random.uniform(jax.random.fold_in(jax.random.fold_in(key, 6), dim), (shards_of,), jnp.float32, low / len(split), top_value / len(split))
        return jnp.repeat(jnp.exp(steps), dims[dim] // shards_of).reshape((-1,) + (1,) * (len(dims) - dim - 1))

    loudness = one(*split[0])
    for cut in split[1:]:
        loudness = loudness * one(*cut)
    return loudness


def gaussian(rng, dims, deviation, reach, cuts=(), kind=jnp.bfloat16):
    array = jax.random.normal(rng, dims, jnp.float32) * deviation
    if len(cuts) > 0:
        array = block_scale(rng, dims, cuts, -0.22, 0.18) * array
    return jnp.clip(array, min=-reach, max=reach).astype(kind)


def setup_inputs(seed: int = 0) -> dict:
    keys = jax.random.split(jax.random.key(seed), 15)
    atmos_state = gaussian(keys[0], (TOKENS, D), 1.0, 6.0, ((0, 8),))
    atmos_gain = jnp.clip(1.0 + 0.15 * jax.random.normal(keys[1], (D,), jnp.float32), 0.25, 1.75)
    w_first = gaussian(keys[2], (D, FF), D ** -0.5, 0.15625, ((0, 8), (1, 4)))
    w_second = gaussian(keys[3], (D, FF), FF ** -0.5, 0.109375, ((0, 8), (1, 4)))
    flux_proj = gaussian(keys[4], (D, C), D ** -0.5, 0.15625)
    remap_index = plant(jax.random.randint(keys[5], (OBLK, KSRC), 0, TOK_DEV // BLK), jax.random.fold_in(keys[5], 1), 0, (TOK_DEV // BLK) - 1).astype(jnp.int32)
    remap_weight = gaussian(keys[6], (OBLK, KSRC, BLK, BLK), (KSRC * BLK) ** -0.5, 0.3125, ((0, 32),))
    ocean_state = gaussian(keys[7], (NXO, NYO, C), 1.0, 6.0, ((0, 8), (1, 4)))
    depth_levels = plant(jax.random.randint(keys[8], (NXO, NYO), 0, LEV + 1), jax.random.fold_in(keys[8], 1), 0, LEV).astype(jnp.int32)
    conv_kernel = gaussian(keys[9], (3, 3, C), 9 ** -0.5, 2.0, (), jnp.float32)
    ocean_gain = jnp.clip(1.0 + 0.15 * jax.random.normal(keys[10], (C,), jnp.float32), 0.25, 1.75)
    ocean_w_in = gaussian(keys[11], (C, HID), C ** -0.5, 0.375)
    ocean_w_out = gaussian(keys[12], (HID, C), HID ** -0.5, 0.1875)
    ocean_cotangent = gaussian(keys[13], (NXO, NYO, C), 1.0, 6.0, ((0, 8), (1, 4)))
    return dict(atmos_state=atmos_state, atmos_gain=atmos_gain, w_first=w_first, w_second=w_second, flux_proj=flux_proj, remap_index=remap_index, remap_weight=remap_weight, ocean_state=ocean_state, depth_levels=depth_levels, conv_kernel=conv_kernel, ocean_gain=ocean_gain, ocean_w_in=ocean_w_in, ocean_w_out=ocean_w_out, ocean_cotangent=ocean_cotangent)


epsilon = 1e-06

def rms_norm(values, gain):
    wide = values.astype(jnp.float32)
    scale = lax.rsqrt(lax.optimization_barrier(jnp.mean(wide * wide, axis=-1, keepdims=True)) + epsilon)
    return (wide * scale * gain).astype(jnp.bfloat16)

def reference(atmos_state, atmos_gain, w_first, w_second, flux_proj, remap_index, remap_weight, ocean_state, depth_levels, conv_kernel, ocean_gain, ocean_w_in, ocean_w_out, ocean_cotangent):
    groups = N_GRP * N_TILE
    share = FF // N_TP

    def atmos_block(block):
        normed = rms_norm(block, atmos_gain)
        total = jnp.zeros((TOK_DEV, D), jnp.float32)
        for q in range(N_TP):
            pre = jnp.dot(normed, w_first[:, q * share:(q + 1) * share], preferred_element_type=jnp.float32)
            hidden = jax.nn.gelu(pre).astype(jnp.bfloat16)
            part = lax.dot_general(hidden, w_second[:, q * share:(q + 1) * share], (((1,), (1,)), ((), ())), preferred_element_type=jnp.float32)
            part = lax.optimization_barrier(part.astype(jnp.bfloat16))
            total = total + part.astype(jnp.float32)
        return (block.astype(jnp.float32) + total).astype(jnp.bfloat16)
    atmos_out = lax.map(atmos_block, atmos_state.reshape(groups, TOK_DEV, D)).reshape(TOKENS, D)
    flux = jnp.dot(atmos_out, flux_proj, preferred_element_type=jnp.float32).astype(jnp.bfloat16)
    flux_blocks = flux.reshape(TOKENS // BLK, BLK, C)
    per_dev = OX * OY // BLK
    rows = jnp.arange(OBLK, dtype=jnp.int32)
    group_of = rows // per_dev // N_TP
    source = (group_of[:, None] * (TOK_DEV // BLK) + remap_index).astype(jnp.int32)

    def remap_one(pair):
        src, weights = pair
        picked = flux_blocks[src].astype(jnp.float32)
        return jnp.einsum('ksr,krc->sc', weights.astype(jnp.float32), picked)
    remapped = lax.map(remap_one, (source, remap_weight)).astype(jnp.bfloat16)
    remapped = remapped.reshape(groups, N_TP, OX, OY, C).transpose(0, 2, 1, 3, 4).reshape(NXO, NYO, C)
    levels = jnp.arange(C, dtype=jnp.int32) // (C // LEV)
    wet = (levels[None, None, :] < depth_levels[:, :, None]).astype(jnp.float32)
    field = ((ocean_state.astype(jnp.float32) + remapped.astype(jnp.float32)) * wet).astype(jnp.bfloat16)
    padded = jnp.pad(field.astype(jnp.float32), ((1, 1), (1, 1), (0, 0)))
    conv = jnp.zeros((NXO, NYO, C), jnp.float32)
    for i in range(3):
        for j in range(3):
            conv = conv + conv_kernel[i, j] * padded[i:i + NXO, j:j + NYO]
    centred = conv - lax.optimization_barrier(jnp.mean(conv, axis=-1, keepdims=True))
    variance = lax.optimization_barrier(jnp.mean(centred * centred, axis=-1, keepdims=True))
    normed = (centred * lax.rsqrt(variance + epsilon) * ocean_gain).astype(jnp.bfloat16)
    cells = NXO * NYO
    step_rows = 4096
    count_blocks = cells // step_rows

    def mlp_block(carry, pieces):
        grad_in, grad_out = carry
        zn, fld, msk, cot = pieces
        pre = jnp.dot(zn, ocean_w_in, preferred_element_type=jnp.float32)
        act, back = jax.vjp(jax.nn.gelu, pre)
        act = act.astype(jnp.bfloat16)
        out = jnp.dot(act, ocean_w_out, preferred_element_type=jnp.float32)
        result = ((fld.astype(jnp.float32) + out) * msk).astype(jnp.bfloat16)
        dout = (cot.astype(jnp.float32) * msk).astype(jnp.bfloat16)
        dact = lax.dot_general(dout, ocean_w_out, (((1,), (1,)), ((), ())), preferred_element_type=jnp.float32)
        dpre = back(dact)[0].astype(jnp.bfloat16)
        grad_in = grad_in + lax.dot_general(dpre, zn, (((0,), (0,)), ((), ())), preferred_element_type=jnp.float32)
        grad_out = grad_out + lax.dot_general(act, dout, (((0,), (0,)), ((), ())), preferred_element_type=jnp.float32)
        return ((grad_in, grad_out), result)
    if cells % step_rows != 0:
        step_rows = cells
        count_blocks = 1
    pieces = (normed.reshape(count_blocks, step_rows, C), field.reshape(count_blocks, step_rows, C), wet.reshape(count_blocks, step_rows, C), ocean_cotangent.reshape(count_blocks, step_rows, C))
    zeros = jnp.zeros((HID, C), jnp.float32)
    (grad_in, grad_out), result = lax.scan(mlp_block, (zeros, zeros), pieces)
    ocean_out = result.reshape(NXO, NYO, C)
    weight_grads = jnp.concatenate([grad_in, grad_out], axis=0)
    return (atmos_out, ocean_out, weight_grads)
```

```python
import jax
import jax.numpy as jnp
from jax import lax
from jax.sharding import PartitionSpec as P

LEV = 16
ALL = ("grp", "tile", "tp")

epsilon = 1e-06
bf16 = jnp.bfloat16
f32 = jnp.float32


def send(value, target):
    groups = lax.axis_size("grp") * lax.axis_size("tile")
    depth = lax.axis_size("tp")
    pairs = []
    for group in range(groups):
        for z in range(depth):
            to = target(group, z)
            if to is not None:
                pairs.append((group * depth + z, to[0] * depth + to[1]))
    return lax.ppermute(value, ALL, pairs)


def flip(mask):
    return lambda group, z: (group ^ mask, z)


def shift_z(step):
    depth = lax.axis_size("tp")
    return lambda group, z: (group, (z + step) % depth)


def next_z(step):
    depth = lax.axis_size("tp")
    return lambda group, z: (group, z + step) if 0 <= z + step < depth else None


def next_group(step):
    groups = lax.axis_size("grp") * lax.axis_size("tile")
    return lambda group, z: (group + step, z) if 0 <= group + step < groups else None


def gather_rows(block):
    groups = lax.axis_size("grp") * lax.axis_size("tile")
    if groups != 8:
        return lax.all_gather(block, ("grp", "tile"), axis=0, tiled=True)
    rows = block.shape[0]
    half = rows // 2
    near = send(block, flip(2))
    side = send(block, flip(4))
    pieces = [(0, 0, block), (1, 0, send(block, flip(1))), (2, 0, near), (4, 0, side)]
    upper = send(side[:half], flip(2))
    lower = send(near[half:], flip(4))
    pieces += [(6, 0, upper), (6, half, lower)]
    pieces += [(3, 0, send(near, flip(1))), (5, 0, send(side, flip(1)))]
    pieces += [(7, 0, send(upper, flip(1))), (7, half, send(lower, flip(1)))]
    me = lax.axis_index(("grp", "tile"))
    full = jnp.zeros((groups * rows, block.shape[1]), block.dtype)
    for mask, offset, piece in pieces:
        full = lax.dynamic_update_slice_in_dim(full, piece, (me ^ mask) * rows + offset, 0)
    return full


def sum_z(parts):
    depth = lax.axis_size("tp")
    arrived = [send(parts(k), shift_z(-k)) for k in range(1, depth)]
    total = parts(0).astype(f32)
    for piece in arrived:
        total = total + piece.astype(f32)
    return total


def scatter_terms(terms):
    ny, nt, depth = lax.axis_size("grp"), lax.axis_size("tile"), lax.axis_size("tp")
    if ny * nt != 8:
        return lax.psum_scatter(terms, ALL, scatter_dimension=0, tiled=True)
    width = terms.shape[1]
    me = lax.axis_index(("grp", "tile"))
    core = me % 2
    place = me // 2
    terms = terms.reshape(4, 2, -1, width)

    def core_part(which):
        return lax.dynamic_index_in_dim(terms, which, 1, keepdims=False)

    terms = core_part(core) + send(core_part(1 - core).astype(bf16), flip(1)).astype(f32)

    def part(mask):
        return lax.dynamic_index_in_dim(terms, place ^ mask, 0, keepdims=False)

    arrived = [send(part(mask).astype(bf16), flip(2 * mask)) for mask in (1, 2, 3)]
    total = part(0)
    for piece in arrived:
        total = total + piece.astype(f32)
    total = total.reshape(depth, -1, width)
    z = lax.axis_index("tp")

    def slab(k):
        piece = lax.dynamic_index_in_dim(total, (z - k) % depth, 0, keepdims=False)
        return piece if k == 0 else piece.astype(bf16)

    return sum_z(slab)


def rms_norm(values, gain):
    wide = values.astype(f32)
    scale = lax.rsqrt(jnp.mean(wide * wide, axis=-1, keepdims=True) + epsilon)
    return (wide * scale * gain).astype(bf16)


def on_device(
    atmos_state,
    atmos_gain,
    w_first,
    w_second,
    flux_proj,
    remap_index,
    remap_weight,
    ocean_state,
    depth_levels,
    conv_kernel,
    ocean_gain,
    ocean_w_in,
    ocean_w_out,
    ocean_cotangent,
):
    depth = lax.axis_size("tp")
    z = lax.axis_index("tp")
    rows_all = atmos_state.shape[0]
    rows_own = rows_all // depth
    block_rows = remap_weight.shape[2]
    channels = flux_proj.shape[1]
    tile_x, tile_y, _ = ocean_state.shape
    cells = tile_x * tile_y
    count = rows_all // block_rows

    full_first = gather_rows(w_first)

    select = (remap_index[:, :, None] == jnp.arange(count, dtype=jnp.int32)).astype(f32)
    matrix = jnp.sum(
        remap_weight.astype(f32)[:, :, :, None, :] * select[:, :, None, :, None], axis=1
    )
    matrix = matrix.astype(bf16).reshape(cells, rows_all)
    matrices = [matrix] + [send(matrix, shift_z(k)) for k in range(1, depth)]

    def column(at):
        state = ocean_state[:, at]
        deep = jnp.broadcast_to(depth_levels[:, at, None].astype(bf16), state.shape)
        return jnp.concatenate([state, deep], axis=0)

    west = send(column(tile_y - 1), next_z(1))
    east = send(column(0), next_z(-1))

    full_second = gather_rows(w_second)

    normed = rms_norm(atmos_state, atmos_gain)
    hsum = jnp.dot(normed, full_first, preferred_element_type=f32)
    hidden = jax.nn.gelu(hsum).astype(bf16)
    partial_sum = lax.dot_general(
        hidden, full_second, (((1,), (1,)), ((), ())), preferred_element_type=f32
    ).astype(bf16)
    flux = jnp.dot(partial_sum, flux_proj, preferred_element_type=f32)
    own_rows = lax.dynamic_slice_in_dim(atmos_state, z * rows_own, rows_own, 0)
    own_flux = jnp.dot(own_rows, flux_proj, preferred_element_type=f32)
    mine = (jnp.arange(depth, dtype=jnp.int32) == z)[:, None, None]
    flux = flux.reshape(depth, rows_own, channels) + jnp.where(mine, own_flux[None], 0.0)
    flux = flux.reshape(rows_all, channels).astype(bf16)

    results = [
        jnp.dot(m, flux, preferred_element_type=f32).astype(bf16).reshape(tile_x, tile_y, channels)
        for m in matrices
    ]

    def remap_part(k):
        return jnp.concatenate(
            [
                results[k].reshape(cells, channels),
                results[(k + 1) % depth][:, tile_y - 1],
                results[(k - 1) % depth][:, 0],
            ],
            axis=0,
        )

    moved = sum_z(remap_part).astype(bf16)

    def atmos_part(k):
        return lax.dynamic_slice_in_dim(partial_sum, ((z - k) % depth) * rows_own, rows_own, 0)

    atmos_out = (own_rows.astype(f32) + sum_z(atmos_part)).astype(bf16)

    levels = jnp.arange(channels, dtype=jnp.int32) // (channels // LEV)
    flat_wet = (levels[None, :] < depth_levels.reshape(cells)[:, None]).astype(f32)
    halo_state = jnp.concatenate([west[:tile_x], east[:tile_x]], axis=0)
    halo_depth = jnp.concatenate([west[tile_x:], east[tile_x:]], axis=0)
    halo_wet = (levels[None, :].astype(f32) < halo_depth.astype(f32)).astype(f32)
    state_all = jnp.concatenate([ocean_state.reshape(cells, channels), halo_state], axis=0)
    wet_all = jnp.concatenate([flat_wet, halo_wet], axis=0)
    field_all = ((state_all.astype(f32) + moved.astype(f32)) * wet_all).astype(bf16)
    flat_field = field_all[:cells]
    middle = jnp.concatenate(
        [
            field_all[cells : cells + tile_x, None],
            flat_field.reshape(tile_x, tile_y, channels),
            field_all[cells + tile_x :, None],
        ],
        axis=1,
    )
    top = send(middle[tile_x - 1 :], next_group(1))
    bottom = send(middle[:1], next_group(-1))
    padded = jnp.concatenate([top, middle, bottom], axis=0).astype(f32)
    conv = jnp.zeros((tile_x, tile_y, channels), f32)
    for i in range(3):
        for j in range(3):
            conv = conv + conv_kernel[i, j] * padded[i : i + tile_x, j : j + tile_y]
    centred = conv - jnp.mean(conv, axis=-1, keepdims=True)
    variance = jnp.mean(centred * centred, axis=-1, keepdims=True)
    ocean_normed = (
        (centred * lax.rsqrt(variance + epsilon) * ocean_gain).astype(bf16).reshape(cells, channels)
    )
    pre = jnp.dot(ocean_normed, ocean_w_in, preferred_element_type=f32)
    activated, backward = jax.vjp(jax.nn.gelu, pre)
    activated = activated.astype(bf16)
    out = jnp.dot(activated, ocean_w_out, preferred_element_type=f32)
    ocean_out = (
        ((flat_field.astype(f32) + out) * flat_wet).astype(bf16).reshape(tile_x, tile_y, channels)
    )
    dout = (ocean_cotangent.reshape(cells, channels).astype(f32) * flat_wet).astype(bf16)
    dact = lax.dot_general(dout, ocean_w_out, (((1,), (1,)), ((), ())), preferred_element_type=f32)
    dpre = backward(dact)[0].astype(bf16)
    grad_in = lax.dot_general(
        dpre, ocean_normed, (((0,), (0,)), ((), ())), preferred_element_type=f32
    )
    grad_out = lax.dot_general(
        activated, dout, (((0,), (0,)), ((), ())), preferred_element_type=f32
    )
    terms = jnp.concatenate([grad_in, grad_out], axis=0)
    return (atmos_out, ocean_out, scatter_terms(terms))


def solution(mesh):
    in_specs = (
        P(("grp", "tile"), None),
        P(),
        P(("grp", "tile"), "tp"),
        P(("grp", "tile"), "tp"),
        P(),
        P(ALL, None),
        P(ALL, None, None, None),
        P(("grp", "tile"), "tp", None),
        P(("grp", "tile"), "tp"),
        P(),
        P(),
        P(),
        P(),
        P(("grp", "tile"), "tp", None),
    )
    out_specs = (
        P(ALL, None),
        P(("grp", "tile"), "tp", None),
        P(ALL, None),
    )
    return jax.shard_map(
        on_device, mesh=mesh, in_specs=in_specs, out_specs=out_specs, check_vma=False
    )
```

```python
import functools

import jax
import jax.numpy as jnp
from jax import lax
from jax.experimental import pallas as pl
from jax.experimental.pallas import tpu as pltpu
from jax.sharding import PartitionSpec as P

LEV = 16
ALL = ("grp", "tile", "tp")

epsilon = 1e-06
bf16 = jnp.bfloat16
f32 = jnp.float32
NT = (((1,), (1,)), ((), ()))
TN = (((0,), (0,)), ((), ()))
VMEM = pl.BlockSpec(memory_space=pltpu.VMEM)
SMEM = pl.BlockSpec(memory_space=pltpu.SMEM)


def send(name, value, target):
    groups = lax.axis_size("grp") * lax.axis_size("tile")
    depth = lax.axis_size("tp")
    pairs = []
    for group in range(groups):
        for z in range(depth):
            to = target(group, z)
            if to is not None:
                pairs.append((group * depth + z, to[0] * depth + to[1]))
    with jax.named_scope(name):
        return lax.ppermute(value, ALL, pairs)


def flip(mask):
    return lambda group, z: (group ^ mask, z)


def shift_z(step):
    depth = lax.axis_size("tp")
    return lambda group, z: (group, (z + step) % depth)


def next_group(step):
    groups = lax.axis_size("grp") * lax.axis_size("tile")
    return lambda group, z: (group + step, z) if 0 <= group + step < groups else None


def gather_rows(name, block):
    groups = lax.axis_size("grp") * lax.axis_size("tile")
    rows = block.shape[0]
    if groups != 8 or rows % 32 != 0:
        full = lax.all_gather(block, ("grp", "tile"), axis=0, tiled=True)
        return [(None, 0, full)]
    half = rows // 2
    core = send(name + "_c", block, flip(1))
    near = send(name + "_x", block, flip(2))
    side = send(name + "_y", block, flip(4))
    upper = send(name + "_yx", side[:half], flip(2))
    lower = send(name + "_xy", near[half:], flip(4))
    return [
        (0, 0, block),
        (1, 0, core),
        (2, 0, near),
        (4, 0, side),
        (3, 0, send(name + "_xc", near, flip(1))),
        (5, 0, send(name + "_yc", side, flip(1))),
        (6, 0, upper),
        (6, half, lower),
        (7, 0, send(name + "_yxc", upper, flip(1))),
        (7, half, send(name + "_xyc", lower, flip(1))),
    ]


def call(body, name, outs, args, specs=None, scratch=(), flops=0, moved=0, tanhs=0):
    return pl.pallas_call(
        body,
        name=name,
        out_shape=[jax.ShapeDtypeStruct(*o) for o in outs],
        in_specs=specs or [VMEM] * len(args),
        out_specs=[VMEM] * len(outs),
        scratch_shapes=list(scratch),
        cost_estimate=pl.CostEstimate(
            flops=int(flops), bytes_accessed=int(moved), transcendentals=int(tanhs)
        ),
        compiler_params=pltpu.CompilerParams(vmem_limit_bytes=56 * 2**20),
    )(*args)


def gelu(x):
    inner = 0.7978845608028654 * (x + 0.044715 * (x * x * x))
    return x * (0.5 * (1.0 + jnp.tanh(inner)))


def gelu_both(x):
    root = 0.7978845608028654
    square = x * x
    t = jnp.tanh(root * (x + 0.044715 * (square * x)))
    half = 0.5 * (1.0 + t)
    slope = half + 0.5 * x * (1.0 - t * t) * (root * (1.0 + 3.0 * 0.044715 * square))
    return x * half, slope


def norm_body(x_ref, gain_ref, out_ref):
    wide = x_ref[...].astype(f32)
    scale = lax.rsqrt(jnp.mean(wide * wide, axis=-1, keepdims=True) + epsilon)
    out_ref[...] = (wide * scale * gain_ref[...]).astype(bf16)


def edge_columns(flat, tile_x, tile_y):
    grid = flat.reshape(tile_x, tile_y, flat.shape[-1])
    return grid[:, 0], grid[:, tile_y - 1]


def matrix_body(tile_x, tile_y, index_ref, weight_ref, state_ref, wet_ref, out_ref):
    blocks, sources, rows, inner = weight_ref.shape
    count = out_ref.shape[1] // inner
    channels = state_ref.shape[1]
    cells = blocks * rows
    for b in range(blocks):
        for j in range(count):
            total = jnp.zeros((rows, inner), f32)
            for k in range(sources):
                hit = jnp.where(index_ref[b, k] == j, 1.0, 0.0).astype(f32)
                total = total + weight_ref[b, k].astype(f32) * hit
            out_ref[b * rows : (b + 1) * rows, j * inner : (j + 1) * inner] = total.astype(bf16)
    first, last = edge_columns(state_ref[...].astype(f32), tile_x, tile_y)
    first_wet, last_wet = edge_columns(wet_ref[...].astype(f32), tile_x, tile_y)
    out_ref[cells:, :channels] = jnp.concatenate([last, last_wet], axis=0).astype(bf16)
    out_ref[cells:, channels:] = jnp.concatenate([first, first_wet], axis=0).astype(bf16)


def place_rows(me, pieces, refs, rows, full_ref):
    for (mask, offset), ref in zip(pieces, refs):
        if mask is None:
            full_ref[...] = ref[...]
        else:
            start = pl.multiple_of((me ^ mask) * rows + offset, 32)
            full_ref[pl.ds(start, ref.shape[0]), :] = ref[...]


def first_body(pieces, rows, depth, id_ref, x_ref, *refs):
    blocks, out_ref, full = refs[:-2], refs[-2], refs[-1]
    place_rows(id_ref[0] // depth, pieces, blocks, rows, full)
    width = out_ref.shape[1]
    step = 256 if width % 256 == 0 else width
    for at in range(0, width, step):
        pre = jnp.dot(x_ref[...], full[:, at : at + step], preferred_element_type=f32)
        out_ref[:, at : at + step] = gelu(pre).astype(bf16)


def second_body(pieces, rows, depth, tile_x, tile_y, id_ref, hid_ref, x_ref, proj_ref, *refs):
    mats, refs = refs[:depth], refs[depth:]
    blocks, refs = refs[: len(pieces)], refs[len(pieces) :]
    parts, moved = refs[:depth], refs[depth : 2 * depth]
    full, sums, flux = refs[2 * depth :]
    me = id_ref[0] // depth
    z = id_ref[0] % depth
    place_rows(me, pieces, blocks, rows, full)
    tokens, width = sums.shape
    own = tokens // depth
    cells = tile_x * tile_y
    step = 256 if width % 256 == 0 else width
    total = jnp.zeros(flux.shape, f32)
    for at in range(0, width, step):
        part = lax.dot_general(
            hid_ref[...], full[at : at + step, :], NT, preferred_element_type=f32
        ).astype(bf16)
        sums[:, at : at + step] = part
        total = total + jnp.dot(part, proj_ref[at : at + step, :], preferred_element_type=f32)
    flux[...] = total
    mine = pl.ds(pl.multiple_of(z * own, own), own)
    flux[mine, :] += jnp.dot(x_ref[mine, :], proj_ref[...], preferred_element_type=f32)
    low = flux[...].astype(bf16)
    results = [jnp.dot(m[:cells, :], low, preferred_element_type=f32) for m in mats]
    edges = [edge_columns(r, tile_x, tile_y) for r in results]
    for k in range(depth):
        moved[k][:cells, :] = results[k].astype(bf16)
        sides = [edges[(k + 1) % depth][1], edges[(k - 1) % depth][0]]
        moved[k][cells:, :] = jnp.concatenate(sides, axis=0).astype(bf16)
    for k in range(depth):
        start = pl.multiple_of(((z - k + depth) % depth) * own, own)
        parts[k][...] = sums[pl.ds(start, own), :]


def field_body(depth, tile_x, tile_y, id_ref, state_ref, wet_ref, west_ref, east_ref, *refs):
    parts, refs = refs[:depth], refs[depth:]
    field_ref, side_ref, first_ref, last_ref = refs
    z = id_ref[0] % depth
    cells = tile_x * tile_y
    channels = state_ref.shape[1]
    total = parts[0][...].astype(f32)
    for p in parts[1:]:
        total = total + p[...].astype(f32)
    total = total.astype(bf16).astype(f32)
    field = ((state_ref[...].astype(f32) + total[:cells]) * wet_ref[...].astype(f32)).astype(bf16)
    field_ref[...] = field
    west = west_ref[cells:, :channels].astype(f32)
    east = east_ref[cells:, channels:].astype(f32)
    open_west = jnp.where(z > 0, 1.0, 0.0).astype(f32)
    open_east = jnp.where(z < depth - 1, 1.0, 0.0).astype(f32)
    side_w = (west[:tile_x] + total[cells : cells + tile_x]) * (west[tile_x:] * open_west)
    side_e = (east[:tile_x] + total[cells + tile_x :]) * (east[tile_x:] * open_east)
    side_ref[...] = jnp.concatenate([side_w, side_e], axis=0).astype(bf16)
    spare = jnp.zeros((first_ref.shape[0] - tile_y - 2, channels), f32)
    wide = field.astype(f32)
    for ref, row in ((first_ref, 0), (last_ref, tile_x - 1)):
        ref[...] = jnp.concatenate(
            [
                wide[row * tile_y : (row + 1) * tile_y],
                side_w[row : row + 1],
                side_e[row : row + 1],
                spare,
            ],
            axis=0,
        ).astype(bf16)


def ocean_body(
    depth, tile_x, tile_y, split, id_ref, field_ref, side_ref, top_ref, low_ref, wet_ref, cot_ref,
    kern_ref, gain_ref, win_ref, wout_ref, *refs
):
    out_ref, refs = refs[0], refs[1:]
    pad = refs[-1]
    cells, channels = field_ref.shape
    core = (id_ref[0] // depth) % 2
    at = 8
    pad[1 : tile_x + 1, at : at + tile_y, :] = (
        field_ref[...].astype(f32).reshape(tile_x, tile_y, channels)
    )
    side = side_ref[...].astype(f32)
    pad[1 : tile_x + 1, at - 1, :] = side[:tile_x]
    pad[1 : tile_x + 1, at + tile_y, :] = side[tile_x:]
    for row, ref in ((0, top_ref), (tile_x + 1, low_ref)):
        line = ref[...].astype(f32)
        pad[row, at : at + tile_y, :] = line[:tile_y]
        pad[row, at - 1 : at, :] = line[tile_y : tile_y + 1]
        pad[row, at + tile_y : at + tile_y + 1, :] = line[tile_y + 1 : tile_y + 2]
    conv = jnp.zeros((tile_x, tile_y, channels), f32)
    for i in range(3):
        for j in range(3):
            tap = kern_ref[i, j].reshape(1, 1, channels)
            conv = conv + tap * pad[i : i + tile_x, at - 1 + j : at - 1 + j + tile_y, :]
    conv = conv.reshape(cells, channels)
    centred = conv - jnp.mean(conv, axis=-1, keepdims=True)
    variance = jnp.mean(centred * centred, axis=-1, keepdims=True)
    normed = (centred * lax.rsqrt(variance + epsilon) * gain_ref[...]).astype(bf16)
    wet = wet_ref[...].astype(f32)
    dout = (cot_ref[...].astype(f32) * wet).astype(bf16)
    hid = win_ref.shape[1]
    step = hid // 4
    total = jnp.zeros((cells, channels), f32)
    for c in range(4):
        span = slice(c * step, (c + 1) * step)
        pre = jnp.dot(normed, win_ref[:, span], preferred_element_type=f32)
        value, slope = gelu_both(pre)
        act = value.astype(bf16)
        total = total + jnp.dot(act, wout_ref[span, :], preferred_element_type=f32)
        dact = lax.dot_general(dout, wout_ref[span, :], NT, preferred_element_type=f32)
        dpre = (dact * slope).astype(bf16)
        grads = (
            lax.dot_general(dpre, normed, TN, preferred_element_type=f32),
            lax.dot_general(act, dout, TN, preferred_element_type=f32),
        )
        for which, grad in enumerate(grads):
            if not split:
                refs[0][which * hid + c * step : which * hid + (c + 1) * step, :] = grad
                continue
            spot = 2 * which + c // 2

            @pl.when(core == c % 2)
            def _():
                refs[0][spot] = grad

            @pl.when(core != c % 2)
            def _():
                refs[1][spot] = grad.astype(bf16)

    out_ref[...] = ((field_ref[...].astype(f32) + total) * wet).astype(bf16)


def plane_body(depth, id_ref, keep_ref, got_ref, own_ref, *outs):
    place = id_ref[0] // depth // 2
    for mask, ref in enumerate((own_ref,) + outs):
        spot = place ^ mask
        ref[...] = (keep_ref[spot] + got_ref[spot].astype(f32)).astype(ref.dtype)


def line_body(depth, id_ref, own_ref, a_ref, b_ref, c_ref, *refs):
    outs, total = refs[:-1], refs[-1]
    z = id_ref[0] % depth
    total[...] = own_ref[...] + a_ref[...].astype(f32) + b_ref[...].astype(f32) + c_ref[...].astype(f32)
    rows = total.shape[0] // depth
    for k, ref in enumerate(outs):
        start = pl.multiple_of(((z - k + depth) % depth) * rows, rows)
        ref[...] = total[pl.ds(start, rows), :].astype(ref.dtype)


def sum_body(*refs):
    out_ref = refs[-1]
    total = refs[0][...].astype(f32)
    for ref in refs[1:-1]:
        total = total + ref[...].astype(f32)
    out_ref[...] = total.astype(out_ref.dtype)


def atmos_body(depth, id_ref, x_ref, *refs):
    out_ref = refs[-1]
    own = out_ref.shape[0]
    z = id_ref[0] % depth
    total = x_ref[pl.ds(pl.multiple_of(z * own, own), own), :].astype(f32)
    for ref in refs[:-1]:
        total = total + ref[...].astype(f32)
    out_ref[...] = total.astype(bf16)


def on_device(
    atmos_state,
    atmos_gain,
    w_first,
    w_second,
    flux_proj,
    remap_index,
    remap_weight,
    ocean_state,
    depth_levels,
    conv_kernel,
    ocean_gain,
    ocean_w_in,
    ocean_w_out,
    ocean_cotangent,
):
    depth = lax.axis_size("tp")
    groups = lax.axis_size("grp") * lax.axis_size("tile")
    me = lax.axis_index(ALL).astype(jnp.int32).reshape(1)
    tokens, model = atmos_state.shape
    own = tokens // depth
    channels = flux_proj.shape[1]
    share = w_first.shape[1]
    tile_x, tile_y, _ = ocean_state.shape
    cells = tile_x * tile_y
    hid = ocean_w_in.shape[1]
    mb = 2**20

    first = gather_rows("wa", w_first)

    levels = jnp.arange(channels, dtype=jnp.int32) // (channels // LEV)
    wet = (levels[None, :] < depth_levels.reshape(cells)[:, None]).astype(bf16)
    state = ocean_state.reshape(cells, channels)
    (matrix,) = call(
        functools.partial(matrix_body, tile_x, tile_y),
        "matrix",
        [((cells + 2 * tile_x, tokens), bf16)],
        (remap_index, remap_weight, state, wet),
        specs=[SMEM, VMEM, VMEM, VMEM],
        moved=mb,
    )
    matrices = [matrix] + [send(f"mat{k}", matrix, shift_z(k)) for k in range(1, depth)]
    (normed,) = call(
        norm_body,
        "norm",
        [((tokens, model), bf16)],
        (atmos_state, atmos_gain.reshape(1, model)),
        moved=3 * mb,
    )

    pieces = [p[:2] for p in first]
    (hidden,) = call(
        functools.partial(first_body, pieces, w_first.shape[0], depth),
        "first",
        [((tokens, share), bf16)],
        (me, normed, *[p[2] for p in first]),
        specs=[SMEM] + [VMEM] * (1 + len(first)),
        scratch=[pltpu.VMEM((model, share), bf16)],
        flops=2 * tokens * model * share,
        moved=5 * mb,
        tanhs=tokens * share,
    )

    second = gather_rows("wb", w_second)
    pieces = [p[:2] for p in second]
    outs = call(
        functools.partial(second_body, pieces, w_second.shape[0], depth, tile_x, tile_y),
        "second",
        [((own, model), bf16)] * depth + [((cells + 2 * tile_x, channels), bf16)] * depth,
        (me, hidden, atmos_state, flux_proj, *matrices, *[p[2] for p in second]),
        specs=[SMEM] + [VMEM] * (3 + depth + len(second)),
        scratch=[
            pltpu.VMEM((model, share), bf16),
            pltpu.VMEM((tokens, model), bf16),
            pltpu.VMEM((tokens, channels), f32),
        ],
        flops=2 * tokens * model * (share + channels),
        moved=8 * mb,
    )
    parts, moved = outs[:depth], outs[depth:]
    moved = [moved[0]] + [send(f"flux{k}", moved[k], shift_z(-k)) for k in range(1, depth)]
    parts = [parts[0]] + [send(f"sum{k}", parts[k], shift_z(-k)) for k in range(1, depth)]

    line = -(-(tile_y + 2) // 16) * 16
    field, side, row_first, row_last = call(
        functools.partial(field_body, depth, tile_x, tile_y),
        "field",
        [((cells, channels), bf16), ((2 * tile_x, channels), bf16)]
        + [((line, channels), bf16)] * 2,
        (me, state, wet, matrices[1], matrices[depth - 1], *moved),
        specs=[SMEM] + [VMEM] * (4 + depth),
        moved=mb,
    )
    top = send("halo_up", row_last, next_group(1))
    low = send("halo_down", row_first, next_group(-1))

    split = groups == 8
    grad_outs = [((2 * hid, channels), f32)]
    if split:
        grad_outs = [((4, hid // 4, channels), f32), ((4, hid // 4, channels), bf16)]
    outs = call(
        functools.partial(ocean_body, depth, tile_x, tile_y, split),
        "ocean",
        [((cells, channels), bf16)] + grad_outs,
        (
            me,
            field,
            side,
            top,
            low,
            wet,
            ocean_cotangent.reshape(cells, channels),
            conv_kernel,
            ocean_gain.reshape(1, channels),
            ocean_w_in,
            ocean_w_out,
        ),
        specs=[SMEM] + [VMEM] * 10,
        scratch=[pltpu.VMEM((tile_x + 2, tile_y + 16, channels), f32)],
        flops=10 * cells * channels * hid,
        moved=5 * mb,
        tanhs=cells * hid,
    )
    ocean_out = outs[0].reshape(tile_x, tile_y, channels)
    if split:
        keep, give = outs[1:]
        got = send("grad_c", give, flip(1))
        rows = hid // 4
        plane = call(
            functools.partial(plane_body, depth),
            "plane",
            [((rows, channels), f32)] + [((rows, channels), bf16)] * 3,
            (me, keep, got),
            specs=[SMEM, VMEM, VMEM],
            moved=2 * mb,
        )
        arrived = [send(f"grad_p{m}", plane[m], flip(2 * m)) for m in (1, 2, 3)]
        rows = rows // depth
        slabs = call(
            functools.partial(line_body, depth),
            "line",
            [((rows, channels), f32)] + [((rows, channels), bf16)] * (depth - 1),
            (me, plane[0], *arrived),
            specs=[SMEM] + [VMEM] * 4,
            scratch=[pltpu.VMEM((rows * depth, channels), f32)],
            moved=mb,
        )
        arrived = [send(f"grad_z{k}", slabs[k], shift_z(-k)) for k in range(1, depth)]
        (weight_grads,) = call(
            sum_body, "grads", [((rows, channels), f32)], (slabs[0], *arrived), moved=mb // 4
        )
    else:
        weight_grads = lax.psum_scatter(outs[1], ALL, scatter_dimension=0, tiled=True)

    (atmos_out,) = call(
        functools.partial(atmos_body, depth),
        "atmos",
        [((own, model), bf16)],
        (me, atmos_state, *parts),
        specs=[SMEM] + [VMEM] * (1 + depth),
        moved=3 * mb,
    )
    return (atmos_out, ocean_out, weight_grads)


def solution(mesh):
    in_specs = (
        P(("grp", "tile"), None),
        P(),
        P(("grp", "tile"), "tp"),
        P(("grp", "tile"), "tp"),
        P(),
        P(ALL, None),
        P(ALL, None, None, None),
        P(("grp", "tile"), "tp", None),
        P(("grp", "tile"), "tp"),
        P(),
        P(),
        P(),
        P(),
        P(("grp", "tile"), "tp", None),
    )
    out_specs = (
        P(ALL, None),
        P(("grp", "tile"), "tp", None),
        P(ALL, None),
    )
    return jax.shard_map(
        on_device, mesh=mesh, in_specs=in_specs, out_specs=out_specs, check_vma=False
    )
```

```python
import functools

import jax
import jax.numpy as jnp
from jax import lax
from jax.experimental import pallas as pl
from jax.experimental.pallas import tpu as pltpu
from jax.sharding import PartitionSpec as P


LEV = 16
ALL = ("grp", "tile", "tp")

epsilon = 1e-06
bf16 = jnp.bfloat16
f32 = jnp.float32
NT = (((1,), (1,)), ((), ()))
TN = (((0,), (0,)), ((), ()))
VMEM = pl.BlockSpec(memory_space=pltpu.VMEM)
SMEM = pl.BlockSpec(memory_space=pltpu.SMEM)


def send(value, target):
    groups = lax.axis_size("grp") * lax.axis_size("tile")
    depth = lax.axis_size("tp")
    pairs = []
    for group in range(groups):
        for z in range(depth):
            to = target(group, z)
            if to is not None:
                pairs.append((group * depth + z, to[0] * depth + to[1]))
    return lax.ppermute(value, ALL, pairs)


def flip(mask):
    return lambda group, z: (group ^ mask, z)


def shift_z(step):
    depth = lax.axis_size("tp")
    return lambda group, z: (group, (z + step) % depth)


def next_group(step):
    groups = lax.axis_size("grp") * lax.axis_size("tile")
    return lambda group, z: (group + step, z) if 0 <= group + step < groups else None


def gather_rows(block, order):
    groups = lax.axis_size("grp") * lax.axis_size("tile")
    rows = block.shape[0]
    if groups != 8 or rows % 64 != 0:
        full = lax.all_gather(block, ("grp", "tile"), axis=0, tiled=True)
        return [(None, full)]
    masks = {"x": 2, "y": 4}
    held = {0: block}
    for axis in "yx":
        held[masks[axis]] = send(block, flip(masks[axis]))
    leg = masks[order[0]]
    held[6] = send(held[leg], flip(6 - leg))
    for mask in (0, 2, 4, 6):
        held[mask + 1] = send(held[mask], flip(1))
    return sorted(held.items())


def call(body, outs, args, specs=None, scratch=(), flops=0, moved=0, tanhs=0):
    return pl.pallas_call(
        body,
        out_shape=[jax.ShapeDtypeStruct(*o) for o in outs],
        in_specs=specs or [VMEM] * len(args),
        out_specs=[VMEM] * len(outs),
        scratch_shapes=list(scratch),
        cost_estimate=pl.CostEstimate(
            flops=int(flops), bytes_accessed=int(moved), transcendentals=int(tanhs)
        ),
        compiler_params=pltpu.CompilerParams(vmem_limit_bytes=56 * 2**20),
    )(*args)


def gelu(x):
    inner = 0.7978845608028654 * (x + 0.044715 * (x * x * x))
    return x * (0.5 * (1.0 + jnp.tanh(inner)))


def gelu_both(x):
    root = 0.7978845608028654
    square = x * x
    t = jnp.tanh(root * (x + 0.044715 * (square * x)))
    half = 0.5 * (1.0 + t)
    slope = half + 0.5 * x * (1.0 - t * t) * (root * (1.0 + 3.0 * 0.044715 * square))
    return x * half, slope


def norm_body(depth, id_ref, x_ref, gain_ref, proj_ref, out_ref, own_ref):
    wide = x_ref[...].astype(f32)
    scale = lax.rsqrt(jnp.mean(wide * wide, axis=-1, keepdims=True) + epsilon)
    out_ref[...] = (wide * scale * gain_ref[...]).astype(bf16)
    own = own_ref.shape[0]
    mine = pl.ds(pl.multiple_of((id_ref[0] % depth) * own, own), own)
    own_ref[...] = jnp.dot(x_ref[mine, :], proj_ref[...], preferred_element_type=f32)


def edge_columns(flat, tile_x, tile_y):
    grid = flat.reshape(tile_x, tile_y, flat.shape[-1])
    return grid[:, 0], grid[:, tile_y - 1]


def payload_rows(sources, rows, tile_x, halves):
    at_index = sources * rows
    at_state = at_index + -(-sources // 16) * 16
    at_depth = at_state + 2 * halves * tile_x
    return at_index, at_state, at_depth, at_depth + 2 * tile_x


def prep_body(tile_x, tile_y, index_ref, weight_ref, state_ref, depth_ref, out_ref):
    sources, rows, inner = weight_ref.shape
    per_block = index_ref.shape[1]
    channels = state_ref.shape[1]
    halves = channels // inner
    at_index, at_state, at_depth, _ = payload_rows(sources, rows, tile_x, halves)
    for n in range(sources):
        out_ref[n * rows : (n + 1) * rows, :] = weight_ref[n]
    row = lax.broadcasted_iota(jnp.int32, (at_state - at_index, inner), 0)
    table = jnp.zeros(row.shape, jnp.int32)
    for n in range(sources):
        table = jnp.where(row == n, index_ref[n // per_block, n % per_block], table)
    out_ref[at_index:at_state, :] = table.astype(f32).astype(bf16)
    first, last = edge_columns(state_ref[...].astype(f32), tile_x, tile_y)
    edges = [e[:, h * inner : (h + 1) * inner] for e in (last, first) for h in range(halves)]
    out_ref[at_state:at_depth, :] = jnp.concatenate(edges, axis=0).astype(bf16)
    deep = depth_ref[...].astype(f32)
    edges = [
        jnp.broadcast_to(deep[:, at : at + 1], (tile_x, inner)) for at in (tile_y - 1, 0)
    ]
    out_ref[at_depth:, :] = jnp.concatenate(edges, axis=0).astype(bf16)


def build_matrix(per_block, sources, rows, at_index, load_ref, out_ref):
    inner = load_ref.shape[1]
    count = out_ref.shape[1] // inner
    for b in range(sources // per_block):
        taken = range(b * per_block, (b + 1) * per_block)
        values = [load_ref[n * rows : (n + 1) * rows, :].astype(f32) for n in taken]
        picks = [load_ref[at_index + n : at_index + n + 1, :].astype(f32) for n in taken]
        for j in range(count):
            total = jnp.zeros((rows, inner), f32)
            for value, pick in zip(values, picks):
                total = total + jnp.where(pick == float(j), 1.0, 0.0) * value
            out_ref[b * rows : (b + 1) * rows, j * inner : (j + 1) * inner] = total.astype(bf16)


def place_rows(me, pieces, refs, rows, full_ref):
    for mask, ref in zip(pieces, refs):
        if mask is None:
            full_ref[...] = ref[...]
        else:
            full_ref[pl.ds(pl.multiple_of((me ^ mask) * rows, 64), rows), :] = ref[...]


def add_product(me, x_ref, pieces, rows, full_ref, at, step, total):
    if pieces[0] is None:
        part = jnp.dot(x_ref[...], full_ref[:, at : at + step], preferred_element_type=f32)
        return part if total is None else total + part
    for n, pair in enumerate(sorted({mask // 2 for mask in pieces})):
        start = pl.multiple_of(((me // 2) ^ pair) * (2 * rows), 128)
        part = jnp.dot(
            x_ref[:, pl.ds(start, 2 * rows)],
            full_ref[n * 2 * rows : (n + 1) * 2 * rows, at : at + step],
            preferred_element_type=f32,
        )
        total = part if total is None else total + part
    return total


def place_pairs(me, pieces, refs, rows, full_ref):
    if pieces[0] is None:
        full_ref[...] = refs[0][...]
        return
    pairs = sorted({mask // 2 for mask in pieces})
    for mask, ref in zip(pieces, refs):
        start = pairs.index(mask // 2) * 2 * rows + ((me % 2) ^ (mask % 2)) * rows
        full_ref[pl.ds(pl.multiple_of(start, 64), rows), :] = ref[...]


def early_body(pieces, rows, depth, id_ref, x_ref, *refs):
    blocks, out_ref, full = refs[:-2], refs[-2], refs[-1]
    me = id_ref[0] // depth
    place_pairs(me, pieces, blocks, rows, full)
    width = out_ref.shape[1]
    step = 256 if width % 256 == 0 else width
    for at in range(0, width, step):
        out_ref[:, at : at + step] = add_product(me, x_ref, pieces, rows, full, at, step, None)


def first_body(
    pieces, rows, depth, tile_x, tile_y, remap, early, id_ref, x_ref, own_ref, both_ref, *refs
):
    mats, refs = refs[:depth], refs[depth:]
    sums, refs = refs[: int(early)], refs[int(early) :]
    blocks, refs = refs[: len(pieces)], refs[len(pieces) :]
    hid_ref, moved, refs = refs[0], refs[1 : depth + 1], refs[depth + 1 :]
    full, flux, dense = refs[0], refs[1], refs[2:]
    me = id_ref[0] // depth
    z = id_ref[0] % depth
    place_pairs(me, pieces, blocks, rows, full)
    for k in range(depth):
        build_matrix(*remap, mats[k], dense[k])
    width = hid_ref.shape[1]
    step = 256 if width % 256 == 0 else width
    total = jnp.zeros(flux.shape, f32)
    for at in range(0, width, step):
        pre = sums[0][:, at : at + step] if early else None
        pre = add_product(me, x_ref, pieces, rows, full, at, step, pre)
        hidden = gelu(pre).astype(bf16)
        hid_ref[:, at : at + step] = hidden
        total = total + lax.dot_general(
            hidden, both_ref[:, at : at + step], NT, preferred_element_type=f32
        )
    flux[...] = total
    own = own_ref.shape[0]
    mine = pl.ds(pl.multiple_of(z * own, own), own)
    flux[mine, :] += own_ref[...]
    low = flux[...].astype(bf16)
    cells = tile_x * tile_y
    results = [jnp.dot(m[...], low, preferred_element_type=f32) for m in dense]
    edges = [edge_columns(r, tile_x, tile_y) for r in results]
    for k in range(depth):
        moved[k][:cells, :] = results[k].astype(bf16)
        sides = [edges[(k + 1) % depth][1], edges[(k - 1) % depth][0]]
        moved[k][cells:, :] = jnp.concatenate(sides, axis=0).astype(bf16)


def both_body(pieces, rows, depth, id_ref, proj_ref, *refs):
    blocks, out_ref, full = refs[:-2], refs[-2], refs[-1]
    place_rows(id_ref[0] // depth, pieces, blocks, rows, full)
    out_ref[...] = lax.dot_general(
        proj_ref[...], full[...], TN, preferred_element_type=f32
    ).astype(bf16)


def second_body(pieces, rows, depth, id_ref, hid_ref, *refs):
    blocks, refs = refs[: len(pieces)], refs[len(pieces) :]
    parts, full, sums = refs[:depth], refs[depth], refs[depth + 1]
    z = id_ref[0] % depth
    place_rows(id_ref[0] // depth, pieces, blocks, rows, full)
    tokens, width = sums.shape
    own = tokens // depth
    step = 256 if width % 256 == 0 else width
    for at in range(0, width, step):
        sums[:, at : at + step] = lax.dot_general(
            hid_ref[...], full[at : at + step, :], NT, preferred_element_type=f32
        ).astype(bf16)
    for k in range(depth):
        start = pl.multiple_of(((z - k + depth) % depth) * own, own)
        parts[k][...] = sums[pl.ds(start, own), :]


def field_body(depth, tile_x, tile_y, rows_at, id_ref, state_ref, wet_ref, west_ref, east_ref, *refs):
    parts, refs = refs[:depth], refs[depth:]
    field_ref, side_ref, first_ref, last_ref = refs
    z = id_ref[0] % depth
    cells = tile_x * tile_y
    channels = state_ref.shape[1]
    total = parts[0][...].astype(f32)
    for p in parts[1:]:
        total = total + p[...].astype(f32)
    total = total.astype(bf16).astype(f32)
    field = ((state_ref[...].astype(f32) + total[:cells]) * wet_ref[...].astype(f32)).astype(bf16)
    field_ref[...] = field
    _, at_state, at_depth, _ = rows_at
    inner = west_ref.shape[1]
    halves = channels // inner
    level = lax.broadcasted_iota(jnp.int32, (tile_x, channels), 1) // (channels // LEV)
    sides = []
    for which, ref, inside in ((0, west_ref, z > 0), (1, east_ref, z < depth - 1)):
        at = at_state + which * halves * tile_x
        state = jnp.concatenate(
            [ref[at + h * tile_x : at + (h + 1) * tile_x, :].astype(f32) for h in range(halves)],
            axis=1,
        )
        at = at_depth + which * tile_x
        deep = jnp.concatenate([ref[at : at + tile_x, :].astype(f32)] * halves, axis=1)
        deep = deep * jnp.where(inside, 1.0, 0.0).astype(f32)
        at = cells + which * tile_x
        sides.append(jnp.where(level.astype(f32) < deep, state + total[at : at + tile_x], 0.0))
    side_w, side_e = sides
    side_ref[...] = jnp.concatenate([side_w, side_e], axis=0).astype(bf16)
    spare = jnp.zeros((first_ref.shape[0] - tile_y - 2, channels), f32)
    wide = field.astype(f32)
    for ref, row in ((first_ref, 0), (last_ref, tile_x - 1)):
        ref[...] = jnp.concatenate(
            [
                wide[row * tile_y : (row + 1) * tile_y],
                side_w[row : row + 1],
                side_e[row : row + 1],
                spare,
            ],
            axis=0,
        ).astype(bf16)


def ocean_body(
    depth, tile_x, tile_y, split, id_ref, field_ref, side_ref, top_ref, low_ref, wet_ref, dout_ref,
    kern_ref, gain_ref, win_ref, wout_ref, *refs
):
    out_ref, refs = refs[0], refs[1:]
    pad = refs[-1]
    cells, channels = field_ref.shape
    core = (id_ref[0] // depth) % 2
    at = 8
    pad[1 : tile_x + 1, at : at + tile_y, :] = (
        field_ref[...].astype(f32).reshape(tile_x, tile_y, channels)
    )
    side = side_ref[...].astype(f32)
    pad[1 : tile_x + 1, at - 1, :] = side[:tile_x]
    pad[1 : tile_x + 1, at + tile_y, :] = side[tile_x:]
    for row, ref in ((0, top_ref), (tile_x + 1, low_ref)):
        line = ref[...].astype(f32)
        pad[row, at : at + tile_y, :] = line[:tile_y]
        pad[row, at - 1 : at, :] = line[tile_y : tile_y + 1]
        pad[row, at + tile_y : at + tile_y + 1, :] = line[tile_y + 1 : tile_y + 2]
    conv = jnp.zeros((tile_x, tile_y, channels), f32)
    for i in range(3):
        for j in range(3):
            tap = kern_ref[i, j].reshape(1, 1, channels)
            conv = conv + tap * pad[i : i + tile_x, at - 1 + j : at - 1 + j + tile_y, :]
    conv = conv.reshape(cells, channels)
    centred = conv - jnp.mean(conv, axis=-1, keepdims=True)
    variance = jnp.mean(centred * centred, axis=-1, keepdims=True)
    normed = (centred * lax.rsqrt(variance + epsilon) * gain_ref[...]).astype(bf16)
    wet = wet_ref[...].astype(f32)
    dout = dout_ref[...]
    hid = win_ref.shape[1]
    step = hid // 4
    total = jnp.zeros((cells, channels), f32)
    for c in range(4):
        span = slice(c * step, (c + 1) * step)
        pre = jnp.dot(normed, win_ref[:, span], preferred_element_type=f32)
        value, slope = gelu_both(pre)
        act = value.astype(bf16)
        total = total + jnp.dot(act, wout_ref[span, :], preferred_element_type=f32)
        dact = lax.dot_general(dout, wout_ref[span, :], NT, preferred_element_type=f32)
        dpre = (dact * slope).astype(bf16)
        grads = (
            lax.dot_general(dpre, normed, TN, preferred_element_type=f32),
            lax.dot_general(act, dout, TN, preferred_element_type=f32),
        )
        for which, grad in enumerate(grads):
            if not split:
                refs[0][which * hid + c * step : which * hid + (c + 1) * step, :] = grad
                continue
            spot = 2 * which + c // 2

            @pl.when(core == c % 2)
            def _():
                refs[0][spot] = grad

            @pl.when(core != c % 2)
            def _():
                refs[1][spot] = grad.astype(bf16)

    out_ref[...] = ((field_ref[...].astype(f32) + total) * wet).astype(bf16)


def step(
    atmos_state,
    atmos_gain,
    w_first,
    w_second,
    flux_proj,
    remap_index,
    remap_weight,
    ocean_state,
    depth_levels,
    conv_kernel,
    ocean_gain,
    ocean_w_in,
    ocean_w_out,
    ocean_cotangent,
):
    depth = lax.axis_size("tp")
    groups = lax.axis_size("grp") * lax.axis_size("tile")
    me = lax.axis_index(ALL).astype(jnp.int32).reshape(1)
    tokens, model = atmos_state.shape
    own = tokens // depth
    channels = flux_proj.shape[1]
    share = w_first.shape[1]
    tile_x, tile_y, _ = ocean_state.shape
    cells = tile_x * tile_y
    hid = ocean_w_in.shape[1]
    mb = 2**20

    second = gather_rows(w_second, "yx")
    first = gather_rows(w_first, "xy")
    own_rows = lax.dynamic_slice_in_dim(atmos_state, (me[0] % depth) * own, own, 0)

    levels = jnp.arange(channels, dtype=jnp.int32) // (channels // LEV)
    wet = (levels[None, :] < depth_levels.reshape(cells)[:, None]).astype(bf16)
    state = ocean_state.reshape(cells, channels)
    blocks, per_block, block_rows, inner = remap_weight.shape
    sources = blocks * per_block
    rows_at = payload_rows(sources, block_rows, tile_x, channels // inner)
    (payload,) = call(
        functools.partial(prep_body, tile_x, tile_y),
        [((rows_at[3], inner), bf16)],
        (remap_index, remap_weight.reshape(sources, block_rows, inner), state, depth_levels),
        specs=[SMEM, VMEM, VMEM, VMEM],
        moved=mb,
    )
    payloads = [payload] + [send(payload, shift_z(k)) for k in range(1, depth)]
    normed, own_flux = call(
        functools.partial(norm_body, depth),
        [((tokens, model), bf16), ((own, channels), f32)],
        (me, atmos_state, atmos_gain.reshape(1, model), flux_proj),
        specs=[SMEM] + [VMEM] * 3,
        moved=4 * mb,
    )

    rows = w_second.shape[0]
    second_at = [p[0] for p in second]
    second = [p[1] for p in second]
    (both,) = call(
        functools.partial(both_body, second_at, rows, depth),
        [((channels, share), bf16)],
        (me, flux_proj, *second),
        specs=[SMEM] + [VMEM] * (1 + len(second)),
        scratch=[pltpu.VMEM((model, share), bf16)],
        flops=2 * model * share * channels,
        moved=3 * mb,
    )

    rows = w_first.shape[0]
    early = first[0][0] is not None
    sums = []
    if early:
        soon = [p for p in first if p[0] < 6]
        first = [p for p in first if p[0] >= 6]
        sums = call(
            functools.partial(early_body, [p[0] for p in soon], rows, depth),
            [((tokens, share), f32)],
            (me, normed, *[p[1] for p in soon]),
            specs=[SMEM] + [VMEM] * (1 + len(soon)),
            scratch=[pltpu.VMEM((6 * rows, share), bf16)],
            flops=2 * tokens * share * 6 * rows,
            moved=5 * mb,
        )
    outs = call(
        functools.partial(
            first_body,
            [p[0] for p in first],
            rows,
            depth,
            tile_x,
            tile_y,
            (per_block, sources, block_rows, rows_at[0]),
            early,
        ),
        [((tokens, share), bf16)] + [((cells + 2 * tile_x, channels), bf16)] * depth,
        (me, normed, own_flux, both, *payloads, *sums, *[p[1] for p in first]),
        specs=[SMEM] + [VMEM] * (3 + depth + len(sums) + len(first)),
        scratch=[
            pltpu.VMEM((2 * rows if early else model, share), bf16),
            pltpu.VMEM((tokens, channels), f32),
        ]
        + [pltpu.VMEM((cells, tokens), bf16)] * depth,
        flops=2 * tokens * share * (2 * rows + channels),
        moved=5 * mb,
        tanhs=tokens * share,
    )
    hidden, moved = outs[0], outs[1:]
    moved = [moved[0]] + [send(moved[k], shift_z(-k)) for k in range(1, depth)]

    rows = w_second.shape[0]
    parts = call(
        functools.partial(second_body, second_at, rows, depth),
        [((own, model), bf16)] * depth,
        (me, hidden, *second),
        specs=[SMEM] + [VMEM] * (1 + len(second)),
        scratch=[pltpu.VMEM((model, share), bf16), pltpu.VMEM((tokens, model), bf16)],
        flops=2 * tokens * model * share,
        moved=6 * mb,
    )
    parts = [parts[0]] + [send(parts[k], shift_z(-k)) for k in range(1, depth)]

    dout = (ocean_cotangent.reshape(cells, channels).astype(f32) * wet.astype(f32)).astype(bf16)

    line = -(-(tile_y + 2) // 16) * 16
    field, side, row_first, row_last = call(
        functools.partial(field_body, depth, tile_x, tile_y, rows_at),
        [((cells, channels), bf16), ((2 * tile_x, channels), bf16)]
        + [((line, channels), bf16)] * 2,
        (me, state, wet, payloads[1], payloads[depth - 1], *moved),
        specs=[SMEM] + [VMEM] * (4 + depth),
        moved=mb,
    )
    top = send(row_last, next_group(1))
    low = send(row_first, next_group(-1))

    split = groups == 8
    grad_outs = [((2 * hid, channels), f32)]
    if split:
        grad_outs = [((4, hid // 4, channels), f32), ((4, hid // 4, channels), bf16)]
    outs = call(
        functools.partial(ocean_body, depth, tile_x, tile_y, split),
        [((cells, channels), bf16)] + grad_outs,
        (
            me,
            field,
            side,
            top,
            low,
            wet,
            dout,
            conv_kernel,
            ocean_gain.reshape(1, channels),
            ocean_w_in,
            ocean_w_out,
        ),
        specs=[SMEM] + [VMEM] * 10,
        scratch=[pltpu.VMEM((tile_x + 2, tile_y + 16, channels), f32)],
        flops=10 * cells * channels * hid,
        moved=5 * mb,
        tanhs=cells * hid,
    )
    ocean_out = outs[0].reshape(tile_x, tile_y, channels)
    if split:
        keep, give = outs[1:]
        place = me[0] // depth // 2

        def quarter(mask):
            return lax.dynamic_index_in_dim(terms, place ^ mask, 0, keepdims=False)

        terms = keep + send(give, flip(1)).astype(f32)
        arrived = [send(quarter(m).astype(bf16), flip(2 * m)) for m in (1, 2, 3)]
        total = quarter(0)
        for piece in arrived:
            total = total + piece.astype(f32)
        total = total.reshape(depth, -1, channels)
        z = me[0] % depth

        def slab(k):
            return lax.dynamic_index_in_dim(total, (z - k) % depth, 0, keepdims=False)

        arrived = [send(slab(k).astype(bf16), shift_z(-k)) for k in range(1, depth)]
        weight_grads = slab(0)
        for piece in arrived:
            weight_grads = weight_grads + piece.astype(f32)
    else:
        weight_grads = lax.psum_scatter(outs[1], ALL, scatter_dimension=0, tiled=True)

    total = own_rows.astype(f32)
    for part in parts:
        total = total + part.astype(f32)
    atmos_out = total.astype(bf16)
    return (atmos_out, ocean_out, weight_grads)


def solution(mesh):
    in_specs = (
        P(("grp", "tile"), None),
        P(),
        P(("grp", "tile"), "tp"),
        P(("grp", "tile"), "tp"),
        P(),
        P(ALL, None),
        P(ALL, None, None, None),
        P(("grp", "tile"), "tp", None),
        P(("grp", "tile"), "tp"),
        P(),
        P(),
        P(),
        P(),
        P(("grp", "tile"), "tp", None),
    )
    out_specs = (
        P(ALL, None),
        P(("grp", "tile"), "tp", None),
        P(ALL, None),
    )
    return jax.shard_map(step, mesh=mesh, in_specs=in_specs, out_specs=out_specs, check_vma=False)
```

```python
import functools

import jax
import jax.numpy as jnp
from jax import lax
from jax.experimental import pallas as pl
from jax.experimental.pallas import tpu as pltpu
from jax.sharding import PartitionSpec as P


LEV = 16
ALL = ("grp", "tile", "tp")

epsilon = 1e-06
bf16 = jnp.bfloat16
f32 = jnp.float32
NT = (((1,), (1,)), ((), ()))
TN = (((0,), (0,)), ((), ()))
VMEM = pl.BlockSpec(memory_space=pltpu.VMEM)
SMEM = pl.BlockSpec(memory_space=pltpu.SMEM)


def send(value, target):
    groups = lax.axis_size("grp") * lax.axis_size("tile")
    depth = lax.axis_size("tp")
    pairs = []
    for group in range(groups):
        for z in range(depth):
            to = target(group, z)
            if to is not None:
                pairs.append((group * depth + z, to[0] * depth + to[1]))
    return lax.ppermute(value, ALL, pairs)


def flip(mask):
    return lambda group, z: (group ^ mask, z)


def shift_z(step):
    depth = lax.axis_size("tp")
    return lambda group, z: (group, (z + step) % depth)


def next_group(step):
    groups = lax.axis_size("grp") * lax.axis_size("tile")
    return lambda group, z: (group + step, z) if 0 <= group + step < groups else None


def gather_rows(block, order):
    groups = lax.axis_size("grp") * lax.axis_size("tile")
    rows = block.shape[0]
    if groups != 8 or rows % 64 != 0:
        full = lax.all_gather(block, ("grp", "tile"), axis=0, tiled=True)
        return [(None, full)]
    masks = {"x": 2, "y": 4}
    held = {0: block}
    for axis in "yx":
        held[masks[axis]] = send(block, flip(masks[axis]))
    leg = masks[order[0]]
    held[6] = send(held[leg], flip(6 - leg))
    for mask in (0, 2, 4, 6):
        held[mask + 1] = send(held[mask], flip(1))
    return sorted(held.items())


def call(body, outs, args, specs=None, scratch=(), flops=0, moved=0, tanhs=0):
    return pl.pallas_call(
        body,
        out_shape=[jax.ShapeDtypeStruct(*o) for o in outs],
        in_specs=specs or [VMEM] * len(args),
        out_specs=[VMEM] * len(outs),
        scratch_shapes=list(scratch),
        cost_estimate=pl.CostEstimate(
            flops=int(flops), bytes_accessed=int(moved), transcendentals=int(tanhs)
        ),
        compiler_params=pltpu.CompilerParams(vmem_limit_bytes=20 * 2**20),
    )(*args)


def gelu(x):
    inner = 0.7978845608028654 * (x + 0.044715 * (x * x * x))
    return x * (0.5 * (1.0 + jnp.tanh(inner)))


def gelu_both(x):
    root = 0.7978845608028654
    square = x * x
    t = jnp.tanh(root * (x + 0.044715 * (square * x)))
    half = 0.5 * (1.0 + t)
    slope = half + 0.5 * x * (1.0 - t * t) * (root * (1.0 + 3.0 * 0.044715 * square))
    return x * half, slope


def norm_body(depth, id_ref, x_ref, gain_ref, proj_ref, out_ref, own_ref):
    wide = x_ref[...].astype(f32)
    scale = lax.rsqrt(jnp.mean(wide * wide, axis=-1, keepdims=True) + epsilon)
    out_ref[...] = (wide * scale * gain_ref[...].reshape(1, -1)).astype(bf16)
    own = own_ref.shape[0]
    mine = pl.ds(pl.multiple_of((id_ref[0] % depth) * own, own), own)
    own_ref[...] = jnp.dot(x_ref[mine, :], proj_ref[...], preferred_element_type=f32)


def edge_columns(flat, tile_x, tile_y):
    grid = flat.reshape(tile_x, tile_y, flat.shape[-1])
    return grid[:, 0], grid[:, tile_y - 1]


def payload_rows(sources, rows, tile_x, halves):
    at_index = sources * rows
    at_state = at_index + -(-sources // 16) * 16
    at_depth = at_state + 2 * halves * tile_x
    return at_index, at_state, at_depth, at_depth + 2 * tile_x


def prep_body(tile_x, tile_y, index_ref, weight_ref, state_ref, depth_ref, out_ref):
    sources, rows, inner = weight_ref.shape
    per_block = index_ref.shape[1]
    channels = state_ref.shape[1]
    halves = channels // inner
    at_index, at_state, at_depth, _ = payload_rows(sources, rows, tile_x, halves)
    for n in range(sources):
        out_ref[n * rows : (n + 1) * rows, :] = weight_ref[n]
    row = lax.broadcasted_iota(jnp.int32, (at_state - at_index, inner), 0)
    table = jnp.zeros(row.shape, jnp.int32)
    for n in range(sources):
        table = jnp.where(row == n, index_ref[n // per_block, n % per_block], table)
    out_ref[at_index:at_state, :] = table.astype(f32).astype(bf16)
    first, last = edge_columns(state_ref[...].astype(f32), tile_x, tile_y)
    edges = [e[:, h * inner : (h + 1) * inner] for e in (last, first) for h in range(halves)]
    out_ref[at_state:at_depth, :] = jnp.concatenate(edges, axis=0).astype(bf16)
    deep = depth_ref[...].astype(f32)
    edges = [
        jnp.broadcast_to(deep[:, at : at + 1], (tile_x, inner)) for at in (tile_y - 1, 0)
    ]
    out_ref[at_depth:, :] = jnp.concatenate(edges, axis=0).astype(bf16)


def build_matrix(per_block, sources, rows, at_index, load_ref, out_ref):
    inner = load_ref.shape[1]
    count = out_ref.shape[1] // inner
    for b in range(sources // per_block):
        taken = range(b * per_block, (b + 1) * per_block)
        values = [load_ref[n * rows : (n + 1) * rows, :].astype(f32) for n in taken]
        picks = [load_ref[at_index + n : at_index + n + 1, :].astype(f32) for n in taken]
        for j in range(count):
            total = jnp.zeros((rows, inner), f32)
            for value, pick in zip(values, picks):
                total = total + jnp.where(pick == float(j), 1.0, 0.0) * value
            out_ref[b * rows : (b + 1) * rows, j * inner : (j + 1) * inner] = total.astype(bf16)


def place_blocks(me, pieces, refs, rows, full_ref, paired):
    pairs = sorted({mask // 2 for mask in pieces if mask is not None})
    for mask, ref in zip(pieces, refs):
        if mask is None:
            full_ref[...] = ref[...]
            continue
        start = (me ^ mask) * rows
        if paired:
            start = pairs.index(mask // 2) * 2 * rows + ((me % 2) ^ (mask % 2)) * rows
        full_ref[pl.ds(pl.multiple_of(start, 64), rows), :] = ref[...]


def add_product(me, x_ref, pieces, rows, full_ref, at, step, total):
    if pieces[0] is None:
        part = jnp.dot(x_ref[...], full_ref[:, at : at + step], preferred_element_type=f32)
        return part if total is None else total + part
    for n, pair in enumerate(sorted({mask // 2 for mask in pieces})):
        start = pl.multiple_of(((me // 2) ^ pair) * (2 * rows), 128)
        part = jnp.dot(
            x_ref[:, pl.ds(start, 2 * rows)],
            full_ref[n * 2 * rows : (n + 1) * 2 * rows, at : at + step],
            preferred_element_type=f32,
        )
        total = part if total is None else total + part
    return total


def early_body(pieces, rows, depth, id_ref, x_ref, *refs):
    blocks, (out_ref, full) = refs[:-2], refs[-2:]
    me = id_ref[0] // depth
    place_blocks(me, pieces, blocks, rows, full, True)
    width = out_ref.shape[1]
    step = 256 if width % 256 == 0 else width
    for at in range(0, width, step):
        out_ref[:, at : at + step] = add_product(me, x_ref, pieces, rows, full, at, step, None)


def first_body(
    pieces, rows, depth, tile_x, tile_y, remap, early, id_ref, x_ref, own_ref, both_ref, *refs
):
    mats, refs = refs[:depth], refs[depth:]
    sums, refs = refs[: int(early)], refs[int(early) :]
    blocks, refs = refs[: len(pieces)], refs[len(pieces) :]
    hid_ref, moved, refs = refs[0], refs[1 : depth + 1], refs[depth + 1 :]
    full, flux, dense = refs[0], refs[1], refs[2:]
    me = id_ref[0] // depth
    z = id_ref[0] % depth
    place_blocks(me, pieces, blocks, rows, full, True)
    for k in range(depth):
        build_matrix(*remap, mats[k], dense[k])
    width = hid_ref.shape[1]
    step = 256 if width % 256 == 0 else width
    total = jnp.zeros(flux.shape, f32)
    for at in range(0, width, step):
        pre = sums[0][:, at : at + step] if early else None
        pre = add_product(me, x_ref, pieces, rows, full, at, step, pre)
        hidden = gelu(pre).astype(bf16)
        hid_ref[:, at : at + step] = hidden
        total = total + lax.dot_general(
            hidden, both_ref[:, at : at + step], NT, preferred_element_type=f32
        )
    flux[...] = total
    own = own_ref.shape[0]
    mine = pl.ds(pl.multiple_of(z * own, own), own)
    flux[mine, :] += own_ref[...]
    low = flux[...].astype(bf16)
    cells = tile_x * tile_y
    results = [jnp.dot(m[...], low, preferred_element_type=f32) for m in dense]
    edges = [edge_columns(r, tile_x, tile_y) for r in results]
    for k in range(depth):
        moved[k][:cells, :] = results[k].astype(bf16)
        sides = [edges[(k + 1) % depth][1], edges[(k - 1) % depth][0]]
        moved[k][cells:, :] = jnp.concatenate(sides, axis=0).astype(bf16)


def both_body(pieces, rows, depth, id_ref, proj_ref, *refs):
    blocks, (out_ref, full) = refs[:-2], refs[-2:]
    place_blocks(id_ref[0] // depth, pieces, blocks, rows, full, False)
    out_ref[...] = lax.dot_general(
        proj_ref[...], full[...], TN, preferred_element_type=f32
    ).astype(bf16)


def second_body(pieces, rows, depth, shards, id_ref, hid_ref, *refs):
    blocks, refs = refs[: len(pieces)], refs[len(pieces) :]
    parts, (full, sums) = refs[:-2], refs[-2:]
    z = id_ref[0] % depth
    place_blocks(id_ref[0] // depth, pieces, blocks, rows, full, False)
    tokens, width = sums.shape
    own = tokens // depth
    step = 256 if width % 256 == 0 else width
    for at in range(0, width, step):
        sums[:, at : at + step] = lax.dot_general(
            hid_ref[...], full[at : at + step, :], NT, preferred_element_type=f32
        ).astype(bf16)
    for ref, rule in zip(parts, shards):
        for n, of in enumerate(rule):
            start = pl.multiple_of(of(z) * own, own)
            ref[n * own : (n + 1) * own, :] = sums[pl.ds(start, own), :]


def field_body(depth, tile_x, tile_y, rows_at, id_ref, state_ref, wet_ref, west_ref, east_ref, *refs):
    parts, refs = refs[:depth], refs[depth:]
    field_ref, side_ref, first_ref, last_ref = refs
    z = id_ref[0] % depth
    cells = tile_x * tile_y
    channels = state_ref.shape[1]
    total = parts[0][...].astype(f32)
    for p in parts[1:]:
        total = total + p[...].astype(f32)
    total = total.astype(bf16).astype(f32)
    field = ((state_ref[...].astype(f32) + total[:cells]) * wet_ref[...].astype(f32)).astype(bf16)
    field_ref[...] = field
    _, at_state, at_depth, _ = rows_at
    inner = west_ref.shape[1]
    halves = channels // inner
    level = lax.broadcasted_iota(jnp.int32, (tile_x, channels), 1) // (channels // LEV)
    sides = []
    for which, ref, inside in ((0, west_ref, z > 0), (1, east_ref, z < depth - 1)):
        at = at_state + which * halves * tile_x
        state = jnp.concatenate(
            [ref[at + h * tile_x : at + (h + 1) * tile_x, :].astype(f32) for h in range(halves)],
            axis=1,
        )
        at = at_depth + which * tile_x
        deep = jnp.concatenate([ref[at : at + tile_x, :].astype(f32)] * halves, axis=1)
        deep = deep * jnp.where(inside, 1.0, 0.0).astype(f32)
        at = cells + which * tile_x
        sides.append(jnp.where(level.astype(f32) < deep, state + total[at : at + tile_x], 0.0))
    side_w, side_e = sides
    side_ref[...] = jnp.concatenate([side_w, side_e], axis=0).astype(bf16)
    spare = jnp.zeros((first_ref.shape[0] - tile_y - 2, channels), f32)
    wide = field.astype(f32)
    for ref, row in ((first_ref, 0), (last_ref, tile_x - 1)):
        ref[...] = jnp.concatenate(
            [
                wide[row * tile_y : (row + 1) * tile_y],
                side_w[row : row + 1],
                side_e[row : row + 1],
                spare,
            ],
            axis=0,
        ).astype(bf16)


def ocean_body(
    depth, tile_x, tile_y, split, id_ref, field_ref, side_ref, top_ref, low_ref, wet_ref, dout_ref,
    kern_ref, gain_ref, win_ref, wout_ref, *refs
):
    out_ref, refs = refs[0], refs[1:]
    pad = refs[-1]
    cells, channels = field_ref.shape
    core = (id_ref[0] // depth) % 2
    at = 8
    pad[1 : tile_x + 1, at : at + tile_y, :] = (
        field_ref[...].astype(f32).reshape(tile_x, tile_y, channels)
    )
    side = side_ref[...].astype(f32)
    pad[1 : tile_x + 1, at - 1, :] = side[:tile_x]
    pad[1 : tile_x + 1, at + tile_y, :] = side[tile_x:]
    for row, ref in ((0, top_ref), (tile_x + 1, low_ref)):
        line = ref[...].astype(f32)
        pad[row, at : at + tile_y, :] = line[:tile_y]
        pad[row, at - 1 : at, :] = line[tile_y : tile_y + 1]
        pad[row, at + tile_y : at + tile_y + 1, :] = line[tile_y + 1 : tile_y + 2]
    conv = jnp.zeros((tile_x, tile_y, channels), f32)
    for i in range(3):
        for j in range(3):
            tap = kern_ref[i, j].reshape(1, 1, channels)
            conv = conv + tap * pad[i : i + tile_x, at - 1 + j : at - 1 + j + tile_y, :]
    conv = conv.reshape(cells, channels)
    centred = conv - jnp.mean(conv, axis=-1, keepdims=True)
    variance = jnp.mean(centred * centred, axis=-1, keepdims=True)
    normed = (centred * lax.rsqrt(variance + epsilon) * gain_ref[...].reshape(1, -1)).astype(bf16)
    wet = wet_ref[...].astype(f32)
    dout = dout_ref[...]
    hid = win_ref.shape[1]
    step = hid // 4
    total = jnp.zeros((cells, channels), f32)
    for c in range(4):
        span = slice(c * step, (c + 1) * step)
        pre = jnp.dot(normed, win_ref[:, span], preferred_element_type=f32)
        value, slope = gelu_both(pre)
        act = value.astype(bf16)
        total = total + jnp.dot(act, wout_ref[span, :], preferred_element_type=f32)
        dact = lax.dot_general(dout, wout_ref[span, :], NT, preferred_element_type=f32)
        dpre = (dact * slope).astype(bf16)
        grads = (
            lax.dot_general(dpre, normed, TN, preferred_element_type=f32),
            lax.dot_general(act, dout, TN, preferred_element_type=f32),
        )
        for which, grad in enumerate(grads):
            if not split:
                refs[0][which * hid + c * step : which * hid + (c + 1) * step, :] = grad
                continue
            spot = 2 * which + c // 2

            @pl.when(core == c % 2)
            def _():
                refs[0][spot] = grad

            @pl.when(core != c % 2)
            def _():
                refs[1][spot] = grad.astype(bf16)

    out_ref[...] = ((field_ref[...].astype(f32) + total) * wet).astype(bf16)


def step(
    atmos_state,
    atmos_gain,
    w_first,
    w_second,
    flux_proj,
    remap_index,
    remap_weight,
    ocean_state,
    depth_levels,
    conv_kernel,
    ocean_gain,
    ocean_w_in,
    ocean_w_out,
    ocean_cotangent,
):
    depth = lax.axis_size("tp")
    groups = lax.axis_size("grp") * lax.axis_size("tile")
    me = lax.axis_index(ALL).astype(jnp.int32).reshape(1)
    tokens, model = atmos_state.shape
    own = tokens // depth
    channels = flux_proj.shape[1]
    share = w_first.shape[1]
    tile_x, tile_y, _ = ocean_state.shape
    cells = tile_x * tile_y
    hid = ocean_w_in.shape[1]
    mb = 2**20

    second = gather_rows(w_second, "yx")
    first = gather_rows(w_first, "xy")
    own_rows = lax.dynamic_slice_in_dim(atmos_state, (me[0] % depth) * own, own, 0)

    levels = jnp.arange(channels, dtype=jnp.int32) // (channels // LEV)
    wet = (levels[None, :] < depth_levels.reshape(cells)[:, None]).astype(bf16)
    state = ocean_state.reshape(cells, channels)
    blocks, per_block, block_rows, inner = remap_weight.shape
    sources = blocks * per_block
    rows_at = payload_rows(sources, block_rows, tile_x, channels // inner)
    (payload,) = call(
        functools.partial(prep_body, tile_x, tile_y),
        [((rows_at[3], inner), bf16)],
        (remap_index, remap_weight.reshape(sources, block_rows, inner), state, depth_levels),
        specs=[SMEM, VMEM, VMEM, VMEM],
        moved=mb,
    )
    payloads = [payload] + [send(payload, shift_z(k)) for k in range(1, depth)]
    normed, own_flux = call(
        functools.partial(norm_body, depth),
        [((tokens, model), bf16), ((own, channels), f32)],
        (me, atmos_state, atmos_gain, flux_proj),
        specs=[SMEM] + [VMEM] * 3,
        moved=4 * mb,
    )

    rows = w_second.shape[0]
    second_at = [p[0] for p in second]
    second = [p[1] for p in second]
    (both,) = call(
        functools.partial(both_body, second_at, rows, depth),
        [((channels, share), bf16)],
        (me, flux_proj, *second),
        specs=[SMEM, VMEM] + [VMEM] * len(second),
        scratch=[pltpu.VMEM((model, share), bf16)],
        flops=2 * model * share * channels,
        moved=3 * mb,
    )

    rows = w_first.shape[0]
    early = first[0][0] is not None
    sums = []
    if early:
        soon = [p for p in first if p[0] < 6]
        first = [p for p in first if p[0] >= 6]
        sums = call(
            functools.partial(early_body, [p[0] for p in soon], rows, depth),
            [((tokens, share), f32)],
            (me, normed, *[p[1] for p in soon]),
            specs=[SMEM, VMEM] + [VMEM] * len(soon),
            scratch=[pltpu.VMEM((6 * rows, share), bf16)],
            flops=2 * tokens * share * 6 * rows,
            moved=5 * mb,
        )
    outs = call(
        functools.partial(
            first_body,
            [p[0] for p in first],
            rows,
            depth,
            tile_x,
            tile_y,
            (per_block, sources, block_rows, rows_at[0]),
            early,
        ),
        [((tokens, share), bf16)] + [((cells + 2 * tile_x, channels), bf16)] * depth,
        (me, normed, own_flux, both, *payloads, *sums, *[p[1] for p in first]),
        specs=[SMEM] + [VMEM] * (3 + depth + len(sums)) + [VMEM] * len(first),
        scratch=[
            pltpu.VMEM((2 * rows if early else model, share), bf16),
            pltpu.VMEM((tokens, channels), f32),
        ]
        + [pltpu.VMEM((cells, tokens), bf16)] * depth,
        flops=2 * tokens * share * (2 * rows + channels),
        moved=5 * mb,
        tanhs=tokens * share,
    )
    hidden, moved = outs[0], outs[1:]
    moved = [moved[0]] + [send(moved[k], shift_z(-k)) for k in range(1, depth)]

    rows = w_second.shape[0]
    pairwise = depth == 4
    if pairwise:
        shards = [
            [lambda z: z],
            [lambda z: z ^ 2],
            [lambda z: z ^ 1, lambda z: z ^ 3],
        ]
    else:
        shards = [[lambda z, k=k: (z - k + depth) % depth] for k in range(depth)]
    parts = call(
        functools.partial(second_body, second_at, rows, depth, shards),
        [((own * len(rule), model), bf16) for rule in shards],
        (me, hidden, *second),
        specs=[SMEM, VMEM] + [VMEM] * len(second),
        scratch=[
            pltpu.VMEM((model, share), bf16),
            pltpu.VMEM((tokens, model), bf16),
        ],
        flops=2 * tokens * model * share,
        moved=6 * mb,
    )
    if pairwise:
        mine, far, give = parts
        got = send(give, lambda group, z: (group, z ^ 1))
        far = (far.astype(f32) + got[own:].astype(f32)).astype(bf16)
        parts = [mine, got[:own], send(far, lambda group, z: (group, z ^ 2))]
    else:
        parts = [parts[0]] + [send(parts[k], shift_z(-k)) for k in range(1, depth)]

    dout = (ocean_cotangent.reshape(cells, channels).astype(f32) * wet.astype(f32)).astype(bf16)

    line = -(-(tile_y + 2) // 16) * 16
    field, side, row_first, row_last = call(
        functools.partial(field_body, depth, tile_x, tile_y, rows_at),
        [((cells, channels), bf16), ((2 * tile_x, channels), bf16)]
        + [((line, channels), bf16)] * 2,
        (me, state, wet, payloads[1], payloads[depth - 1], *moved),
        specs=[SMEM] + [VMEM] * (4 + depth),
        moved=mb,
    )
    top = send(row_last, next_group(1))
    low = send(row_first, next_group(-1))

    split = groups == 8
    grad_outs = [((2 * hid, channels), f32)]
    if split:
        grad_outs = [((4, hid // 4, channels), f32), ((4, hid // 4, channels), bf16)]
    outs = call(
        functools.partial(ocean_body, depth, tile_x, tile_y, split),
        [((cells, channels), bf16)] + grad_outs,
        (
            me,
            field,
            side,
            top,
            low,
            wet,
            dout,
            conv_kernel,
            ocean_gain,
            ocean_w_in,
            ocean_w_out,
        ),
        specs=[SMEM] + [VMEM] * 10,
        scratch=[pltpu.VMEM((tile_x + 2, tile_y + 16, channels), f32)],
        flops=10 * cells * channels * hid,
        moved=5 * mb,
        tanhs=cells * hid,
    )
    ocean_out = outs[0].reshape(tile_x, tile_y, channels)
    if split:
        keep, give = outs[1:]
        place = me[0] // depth // 2

        def quarter(mask):
            return lax.dynamic_index_in_dim(terms, place ^ mask, 0, keepdims=False)

        terms = keep + send(give, flip(1)).astype(f32)
        arrived = [send(quarter(m).astype(bf16), flip(2 * m)) for m in (1, 2, 3)]
        total = quarter(0)
        for piece in arrived:
            total = total + piece.astype(f32)
        total = total.reshape(depth, -1, channels)
        z = me[0] % depth

        def slab(k):
            return lax.dynamic_index_in_dim(total, (z - k) % depth, 0, keepdims=False)

        arrived = [send(slab(k).astype(bf16), shift_z(-k)) for k in range(1, depth)]
        weight_grads = slab(0)
        for piece in arrived:
            weight_grads = weight_grads + piece.astype(f32)
    else:
        weight_grads = lax.psum_scatter(outs[1], ALL, scatter_dimension=0, tiled=True)

    total = own_rows.astype(f32)
    for part in parts:
        total = total + part.astype(f32)
    atmos_out = total.astype(bf16)
    return (atmos_out, ocean_out, weight_grads)


def solution(mesh):
    in_specs = (
        P(("grp", "tile"), None),
        P(),
        P(("grp", "tile"), "tp"),
        P(("grp", "tile"), "tp"),
        P(),
        P(ALL, None),
        P(ALL, None, None, None),
        P(("grp", "tile"), "tp", None),
        P(("grp", "tile"), "tp"),
        P(),
        P(),
        P(),
        P(),
        P(("grp", "tile"), "tp", None),
    )
    out_specs = (
        P(ALL, None),
        P(("grp", "tile"), "tp", None),
        P(ALL, None),
    )
    return jax.shard_map(step, mesh=mesh, in_specs=in_specs, out_specs=out_specs, check_vma=False)
```

```python
import functools

import jax
import jax.numpy as jnp
from jax import lax
from jax.experimental import pallas as pl
from jax.experimental.pallas import tpu as pltpu
from jax.sharding import PartitionSpec as P


LEV = 16
ALL = ("grp", "tile", "tp")

epsilon = 1e-06
bf16 = jnp.bfloat16
f32 = jnp.float32
NT = (((1,), (1,)), ((), ()))
TN = (((0,), (0,)), ((), ()))
VMEM = pl.BlockSpec(memory_space=pltpu.VMEM)
SMEM = pl.BlockSpec(memory_space=pltpu.SMEM)


def send(value, target):
    groups = lax.axis_size("grp") * lax.axis_size("tile")
    depth = lax.axis_size("tp")
    pairs = []
    for group in range(groups):
        for z in range(depth):
            to = target(group, z)
            if to is not None:
                pairs.append((group * depth + z, to[0] * depth + to[1]))
    return lax.ppermute(value, ALL, pairs)


def flip(mask):
    return lambda group, z: (group ^ mask, z)


def shift_z(step):
    depth = lax.axis_size("tp")
    return lambda group, z: (group, (z + step) % depth)


def next_group(step):
    groups = lax.axis_size("grp") * lax.axis_size("tile")
    return lambda group, z: (group + step, z) if 0 <= group + step < groups else None


def gather_rows(block, order):
    groups = lax.axis_size("grp") * lax.axis_size("tile")
    rows = block.shape[0]
    if groups != 8 or rows % 64 != 0:
        full = lax.all_gather(block, ("grp", "tile"), axis=0, tiled=True)
        return [(None, full)]
    masks = {"x": 2, "y": 4}
    held = {0: block}
    for axis in "yx":
        held[masks[axis]] = send(block, flip(masks[axis]))
    leg = masks[order[0]]
    held[6] = send(held[leg], flip(6 - leg))
    for mask in (0, 2, 4, 6):
        held[mask + 1] = send(held[mask], flip(1))
    return sorted(held.items())


def call(body, outs, args, specs=None, scratch=(), flops=0, moved=0, tanhs=0, grant=20):
    return pl.pallas_call(
        body,
        out_shape=[jax.ShapeDtypeStruct(*o) for o in outs],
        in_specs=specs or [VMEM] * len(args),
        out_specs=[VMEM] * len(outs),
        scratch_shapes=list(scratch),
        cost_estimate=pl.CostEstimate(
            flops=int(flops), bytes_accessed=int(moved), transcendentals=int(tanhs)
        ),
        compiler_params=pltpu.CompilerParams(vmem_limit_bytes=grant * 2**20),
    )(*args)


def gelu(x):
    inner = 0.7978845608028654 * (x + 0.044715 * (x * x * x))
    return x * (0.5 * (1.0 + jnp.tanh(inner)))


def gelu_both(x):
    root = 0.7978845608028654
    square = x * x
    t = jnp.tanh(root * (x + 0.044715 * (square * x)))
    half = 0.5 * (1.0 + t)
    slope = half + 0.5 * x * (1.0 - t * t) * (root * (1.0 + 3.0 * 0.044715 * square))
    return x * half, slope


def norm_body(depth, id_ref, x_ref, gain_ref, out_ref, own_ref):
    wide = x_ref[...].astype(f32)
    scale = lax.rsqrt(jnp.mean(wide * wide, axis=-1, keepdims=True) + epsilon)
    out_ref[...] = (wide * scale * gain_ref[...].reshape(1, -1)).astype(bf16)
    own = own_ref.shape[0]
    own_ref[...] = x_ref[pl.ds(pl.multiple_of((id_ref[0] % depth) * own, own), own), :]


def edge_columns(flat, tile_x, tile_y):
    grid = flat.reshape(tile_x, tile_y, flat.shape[-1])
    return grid[:, 0], grid[:, tile_y - 1]


def edge_rows(sources, tile_x, halves):
    at_state = -(-sources // 16) * 16
    at_depth = at_state + 2 * halves * tile_x
    return at_state, at_depth, at_depth + 2 * tile_x


def prep_body(index_ref, state_ref, depth_ref, out_ref, wet_ref):
    tile_x, tile_y = depth_ref.shape
    blocks, per_block = index_ref.shape
    inner = out_ref.shape[1]
    channels = state_ref.shape[1]
    halves = channels // inner
    at_state, at_depth, _ = edge_rows(blocks * per_block, tile_x, halves)
    row = lax.broadcasted_iota(jnp.int32, (at_state, inner), 0)
    table = jnp.zeros(row.shape, jnp.int32)
    for b in range(blocks):
        for k in range(per_block):
            table = jnp.where(row == b * per_block + k, index_ref[b, k], table)
    out_ref[:at_state, :] = table.astype(f32).astype(bf16)
    first, last = edge_columns(state_ref[...].astype(f32), tile_x, tile_y)
    edges = [e[:, h * inner : (h + 1) * inner] for e in (last, first) for h in range(halves)]
    out_ref[at_state:at_depth, :] = jnp.concatenate(edges, axis=0).astype(bf16)
    deep = depth_ref[...].astype(f32)
    edges = [
        jnp.broadcast_to(deep[:, at : at + 1], (tile_x, inner)) for at in (tile_y - 1, 0)
    ]
    out_ref[at_depth:, :] = jnp.concatenate(edges, axis=0).astype(bf16)
    level = lax.broadcasted_iota(jnp.int32, (tile_y, channels), 1) // (channels // LEV)
    down = deep.T
    for x in range(tile_x):
        wet = jnp.where(level.astype(f32) < down[:, x : x + 1], 1.0, 0.0)
        wet_ref[x * tile_y : (x + 1) * tile_y, :] = wet.astype(bf16)


def build_matrix(blocks, weight_ref, edge_ref, out_ref):
    sources, rows, inner = weight_ref.shape
    per_block = sources // blocks
    count = out_ref.shape[1] // inner
    for b in range(blocks):
        taken = range(b * per_block, (b + 1) * per_block)
        values = [weight_ref[n].astype(f32) for n in taken]
        picks = [edge_ref[n : n + 1, :].astype(f32) for n in taken]
        for j in range(count):
            total = jnp.zeros((rows, inner), f32)
            for value, pick in zip(values, picks):
                total = total + jnp.where(pick == float(j), 1.0, 0.0) * value
            out_ref[b * rows : (b + 1) * rows, j * inner : (j + 1) * inner] = total.astype(bf16)


def place_blocks(me, pieces, refs, rows, full_ref, paired):
    pairs = sorted({mask // 2 for mask in pieces if mask is not None})
    for mask, ref in zip(pieces, refs):
        if mask is None:
            full_ref[...] = ref[...]
            continue
        start = (me ^ mask) * rows
        if paired:
            start = pairs.index(mask // 2) * 2 * rows + ((me % 2) ^ (mask % 2)) * rows
        full_ref[pl.ds(pl.multiple_of(start, 64), rows), :] = ref[...]


def add_product(me, x_ref, pieces, rows, full_ref, at, step, total):
    if pieces[0] is None:
        part = jnp.dot(x_ref[...], full_ref[:, at : at + step], preferred_element_type=f32)
        return part if total is None else total + part
    for n, pair in enumerate(sorted({mask // 2 for mask in pieces})):
        start = pl.multiple_of(((me // 2) ^ pair) * (2 * rows), 128)
        part = jnp.dot(
            x_ref[:, pl.ds(start, 2 * rows)],
            full_ref[n * 2 * rows : (n + 1) * 2 * rows, at : at + step],
            preferred_element_type=f32,
        )
        total = part if total is None else total + part
    return total


def early_body(pieces, rows, depth, id_ref, x_ref, *refs):
    blocks, (out_ref, full) = refs[:-2], refs[-2:]
    me = id_ref[0] // depth
    place_blocks(me, pieces, blocks, rows, full, True)
    width = out_ref.shape[1]
    step = 256 if width % 256 == 0 else width
    for at in range(0, width, step):
        out_ref[:, at : at + step] = add_product(me, x_ref, pieces, rows, full, at, step, None)


def first_body(
    pieces, rows, depth, tile_x, tile_y, remap, early, id_ref, x_ref, own_ref, both_ref, *refs
):
    mats, tables, refs = refs[:depth], refs[depth : 2 * depth], refs[2 * depth :]
    sums, refs = refs[: int(early)], refs[int(early) :]
    blocks, refs = refs[: len(pieces)], refs[len(pieces) :]
    hid_ref, moved, refs = refs[0], refs[1 : depth + 1], refs[depth + 1 :]
    full, flux, dense = refs[0], refs[1], refs[2:]
    me = id_ref[0] // depth
    z = id_ref[0] % depth
    place_blocks(me, pieces, blocks, rows, full, True)
    for k in range(depth):
        build_matrix(remap, mats[k], tables[k], dense[k])
    width = hid_ref.shape[1]
    step = 256 if width % 256 == 0 else width
    total = jnp.zeros(flux.shape, f32)
    for at in range(0, width, step):
        pre = sums[0][:, at : at + step] if early else None
        pre = add_product(me, x_ref, pieces, rows, full, at, step, pre)
        hidden = gelu(pre).astype(bf16)
        hid_ref[:, at : at + step] = hidden
        total = total + lax.dot_general(
            hidden, both_ref[:, at : at + step], NT, preferred_element_type=f32
        )
    flux[...] = total
    own = own_ref.shape[0]
    mine = pl.ds(pl.multiple_of(z * own, own), own)
    flux[mine, :] += own_ref[...]
    low = flux[...].astype(bf16)
    cells = tile_x * tile_y
    results = [jnp.dot(m[...], low, preferred_element_type=f32) for m in dense]
    edges = [edge_columns(r, tile_x, tile_y) for r in results]
    for k in range(depth):
        moved[k][:cells, :] = results[k].astype(bf16)
        sides = [edges[(k + 1) % depth][1], edges[(k - 1) % depth][0]]
        moved[k][cells:, :] = jnp.concatenate(sides, axis=0).astype(bf16)


def both_body(pieces, rows, depth, id_ref, proj_ref, own_ref, *refs):
    blocks, (out_ref, flux_ref, full) = refs[:-3], refs[-3:]
    place_blocks(id_ref[0] // depth, pieces, blocks, rows, full, False)
    out_ref[...] = lax.dot_general(
        proj_ref[...], full[...], TN, preferred_element_type=f32
    ).astype(bf16)
    flux_ref[...] = jnp.dot(own_ref[...], proj_ref[...], preferred_element_type=f32)


def back_body(wet_ref, cot_ref, wout_ref, dout_ref, dact_ref):
    dout = (cot_ref[...].astype(f32) * wet_ref[...].astype(f32)).astype(bf16)
    dout_ref[...] = dout
    step = dact_ref.shape[1] // 4
    for at in range(0, dact_ref.shape[1], step):
        dact_ref[:, at : at + step] = lax.dot_general(
            dout, wout_ref[at : at + step, :], NT, preferred_element_type=f32
        )


def second_body(pieces, rows, depth, shards, id_ref, hid_ref, *refs):
    blocks, refs = refs[: len(pieces)], refs[len(pieces) :]
    parts, (full, sums) = refs[:-2], refs[-2:]
    z = id_ref[0] % depth
    place_blocks(id_ref[0] // depth, pieces, blocks, rows, full, False)
    tokens, width = sums.shape
    own = tokens // depth
    step = 256 if width % 256 == 0 else width
    for at in range(0, width, step):
        sums[:, at : at + step] = lax.dot_general(
            hid_ref[...], full[at : at + step, :], NT, preferred_element_type=f32
        ).astype(bf16)
    for ref, rule in zip(parts, shards):
        for n, of in enumerate(rule):
            start = pl.multiple_of(of(z) * own, own)
            ref[n * own : (n + 1) * own, :] = sums[pl.ds(start, own), :]


def field_body(depth, tile_x, tile_y, rows_at, id_ref, state_ref, wet_ref, west_ref, east_ref, *refs):
    parts, refs = refs[:depth], refs[depth:]
    field_ref, side_ref, first_ref, last_ref = refs
    z = id_ref[0] % depth
    cells = tile_x * tile_y
    channels = state_ref.shape[1]
    total = parts[0][...].astype(f32)
    for p in parts[1:]:
        total = total + p[...].astype(f32)
    total = total.astype(bf16).astype(f32)
    field = ((state_ref[...].astype(f32) + total[:cells]) * wet_ref[...].astype(f32)).astype(bf16)
    field_ref[...] = field
    at_state, at_depth, _ = rows_at
    inner = west_ref.shape[1]
    halves = channels // inner
    level = lax.broadcasted_iota(jnp.int32, (tile_x, channels), 1) // (channels // LEV)
    sides = []
    for which, ref, inside in ((0, west_ref, z > 0), (1, east_ref, z < depth - 1)):
        at = at_state + which * halves * tile_x
        state = jnp.concatenate(
            [ref[at + h * tile_x : at + (h + 1) * tile_x, :].astype(f32) for h in range(halves)],
            axis=1,
        )
        at = at_depth + which * tile_x
        deep = jnp.concatenate([ref[at : at + tile_x, :].astype(f32)] * halves, axis=1)
        deep = deep * jnp.where(inside, 1.0, 0.0).astype(f32)
        at = cells + which * tile_x
        sides.append(jnp.where(level.astype(f32) < deep, state + total[at : at + tile_x], 0.0))
    side_w, side_e = sides
    side_ref[...] = jnp.concatenate([side_w, side_e], axis=0).astype(bf16)
    spare = jnp.zeros((first_ref.shape[0] - tile_y - 2, channels), f32)
    wide = field.astype(f32)
    for ref, row in ((first_ref, 0), (last_ref, tile_x - 1)):
        ref[...] = jnp.concatenate(
            [
                wide[row * tile_y : (row + 1) * tile_y],
                side_w[row : row + 1],
                side_e[row : row + 1],
                spare,
            ],
            axis=0,
        ).astype(bf16)


def ocean_body(
    depth, tile_x, tile_y, split, id_ref, field_ref, side_ref, top_ref, low_ref, wet_ref, dout_ref, dact_ref,
    kern_ref, gain_ref, win_ref, wout_ref, *refs
):
    out_ref, refs = refs[0], refs[1:]
    pad = refs[-1]
    cells, channels = field_ref.shape
    core = (id_ref[0] // depth) % 2
    at = 8
    pad[1 : tile_x + 1, at : at + tile_y, :] = (
        field_ref[...].astype(f32).reshape(tile_x, tile_y, channels)
    )
    side = side_ref[...].astype(f32)
    pad[1 : tile_x + 1, at - 1, :] = side[:tile_x]
    pad[1 : tile_x + 1, at + tile_y, :] = side[tile_x:]
    for row, ref in ((0, top_ref), (tile_x + 1, low_ref)):
        line = ref[...].astype(f32)
        pad[row, at : at + tile_y, :] = line[:tile_y]
        pad[row, at - 1 : at, :] = line[tile_y : tile_y + 1]
        pad[row, at + tile_y : at + tile_y + 1, :] = line[tile_y + 1 : tile_y + 2]
    conv = jnp.zeros((tile_x, tile_y, channels), f32)
    for i in range(3):
        for j in range(3):
            tap = kern_ref[i, j].reshape(1, 1, channels)
            conv = conv + tap * pad[i : i + tile_x, at - 1 + j : at - 1 + j + tile_y, :]
    conv = conv.reshape(cells, channels)
    centred = conv - jnp.mean(conv, axis=-1, keepdims=True)
    variance = jnp.mean(centred * centred, axis=-1, keepdims=True)
    normed = (centred * lax.rsqrt(variance + epsilon) * gain_ref[...].reshape(1, -1)).astype(bf16)
    wet = wet_ref[...].astype(f32)
    dout = dout_ref[...]
    hid = win_ref.shape[1]
    step = hid // 4
    total = jnp.zeros((cells, channels), f32)
    for c in range(4):
        span = slice(c * step, (c + 1) * step)
        pre = jnp.dot(normed, win_ref[:, span], preferred_element_type=f32)
        value, slope = gelu_both(pre)
        act = value.astype(bf16)
        total = total + jnp.dot(act, wout_ref[span, :], preferred_element_type=f32)
        dpre = (dact_ref[:, span] * slope).astype(bf16)
        grads = (
            lax.dot_general(dpre, normed, TN, preferred_element_type=f32),
            lax.dot_general(act, dout, TN, preferred_element_type=f32),
        )
        for which, grad in enumerate(grads):
            if not split:
                refs[0][which * hid + c * step : which * hid + (c + 1) * step, :] = grad
                continue
            spot = 2 * which + c // 2

            @pl.when(core == c % 2)
            def _():
                refs[0][spot] = grad

            @pl.when(core != c % 2)
            def _():
                refs[1][spot] = grad.astype(bf16)

    out_ref[...] = ((field_ref[...].astype(f32) + total) * wet).astype(bf16)


def plane_body(depth, id_ref, keep_ref, got_ref, own_ref, *outs):
    place = id_ref[0] // depth // 2
    for mask, ref in enumerate((own_ref,) + outs):
        spot = place ^ mask
        ref[...] = (keep_ref[spot] + got_ref[spot].astype(f32)).astype(ref.dtype)


def line_body(depth, id_ref, own_ref, a_ref, b_ref, c_ref, *refs):
    outs, total = refs[:-1], refs[-1]
    z = id_ref[0] % depth
    arrived = a_ref[...].astype(f32) + b_ref[...].astype(f32) + c_ref[...].astype(f32)
    total[...] = own_ref[...] + arrived
    rows = total.shape[0] // depth
    for k, ref in enumerate(outs):
        start = pl.multiple_of(((z - k + depth) % depth) * rows, rows)
        ref[...] = total[pl.ds(start, rows), :].astype(ref.dtype)


def sum_body(*refs):
    out_ref = refs[-1]
    total = refs[0][...].astype(f32)
    for ref in refs[1:-1]:
        total = total + ref[...].astype(f32)
    out_ref[...] = total.astype(out_ref.dtype)


def step(
    atmos_state,
    atmos_gain,
    w_first,
    w_second,
    flux_proj,
    remap_index,
    remap_weight,
    ocean_state,
    depth_levels,
    conv_kernel,
    ocean_gain,
    ocean_w_in,
    ocean_w_out,
    ocean_cotangent,
):
    depth = lax.axis_size("tp")
    groups = lax.axis_size("grp") * lax.axis_size("tile")
    me = lax.axis_index(ALL).astype(jnp.int32).reshape(1)
    tokens, model = atmos_state.shape
    own = tokens // depth
    channels = flux_proj.shape[1]
    share = w_first.shape[1]
    tile_x, tile_y, _ = ocean_state.shape
    cells = tile_x * tile_y
    hid = ocean_w_in.shape[1]
    mb = 2**20

    second = gather_rows(w_second, "yx")
    first = gather_rows(w_first, "xy")
    state = ocean_state.reshape(cells, channels)
    blocks, per_block, block_rows, inner = remap_weight.shape
    rows_at = edge_rows(blocks * per_block, tile_x, channels // inner)
    weights = remap_weight.reshape(blocks * per_block, block_rows, inner)
    steps = range(1, depth)
    mats = [weights] + [send(weights, shift_z(k)) for k in steps]
    edge, wet = call(
        prep_body,
        [((rows_at[2], inner), bf16), ((cells, channels), bf16)],
        (remap_index, state, depth_levels),
        specs=[SMEM, VMEM, VMEM],
        moved=mb,
    )
    edges = [edge] + [send(edge, shift_z(k)) for k in steps]
    normed, own_rows = call(
        functools.partial(norm_body, depth),
        [((tokens, model), bf16), ((own, model), bf16)],
        (me, atmos_state, atmos_gain),
        specs=[SMEM, VMEM, VMEM],
        moved=4 * mb,
    )

    rows = w_second.shape[0]
    second_at = [p[0] for p in second]
    second = [p[1] for p in second]
    both, own_flux = call(
        functools.partial(both_body, second_at, rows, depth),
        [((channels, share), bf16), ((own, channels), f32)],
        (me, flux_proj, own_rows, *second),
        specs=[SMEM, VMEM, VMEM] + [VMEM] * len(second),
        scratch=[pltpu.VMEM((model, share), bf16)],
        flops=2 * model * share * channels,
        moved=3 * mb,
    )

    rows = w_first.shape[0]
    early = first[0][0] is not None
    sums = []
    if early:
        soon = [p for p in first if p[0] < 6]
        first = [p for p in first if p[0] >= 6]
        sums = call(
            functools.partial(early_body, [p[0] for p in soon], rows, depth),
            [((tokens, share), f32)],
            (me, normed, *[p[1] for p in soon]),
            specs=[SMEM, VMEM] + [VMEM] * len(soon),
            scratch=[pltpu.VMEM((6 * rows, share), bf16)],
            flops=2 * tokens * share * 6 * rows,
            moved=5 * mb,
        )
    outs = call(
        functools.partial(
            first_body,
            [p[0] for p in first],
            rows,
            depth,
            tile_x,
            tile_y,
            blocks,
            early,
        ),
        [((tokens, share), bf16)] + [((cells + 2 * tile_x, channels), bf16)] * depth,
        (me, normed, own_flux, both, *mats, *edges, *sums, *[p[1] for p in first]),
        specs=[SMEM] + [VMEM] * (3 + 2 * depth + len(sums)) + [VMEM] * len(first),
        scratch=[
            pltpu.VMEM((2 * rows if early else model, share), bf16),
            pltpu.VMEM((tokens, channels), f32),
        ]
        + [pltpu.VMEM((cells, tokens), bf16)] * depth,
        flops=2 * tokens * share * (2 * rows + channels),
        moved=5 * mb,
        tanhs=tokens * share,
    )
    hidden, moved = outs[0], outs[1:]
    moved = [moved[0]] + [send(moved[k], shift_z(-k)) for k in range(1, depth)]

    rows = w_second.shape[0]
    pairwise = depth == 4
    if pairwise:
        shards = [
            [lambda z: z],
            [lambda z: z ^ 2],
            [lambda z: z ^ 3],
            [lambda z: z ^ 1],
        ]
    else:
        shards = [[lambda z, k=k: (z - k + depth) % depth] for k in range(depth)]
    parts = call(
        functools.partial(second_body, second_at, rows, depth, shards),
        [((own * len(rule), model), bf16) for rule in shards],
        (me, hidden, *second),
        specs=[SMEM, VMEM] + [VMEM] * len(second),
        scratch=[
            pltpu.VMEM((model, share), bf16),
            pltpu.VMEM((tokens, model), bf16),
        ],
        flops=2 * tokens * model * share,
        moved=6 * mb,
    )
    if pairwise:
        mine, far, give_far, give_near = parts
        near_z = lambda group, z: (group, z ^ 1)
        got_far = send(give_far, near_z)
        got_near = send(give_near, near_z)
        (far,) = call(sum_body, [((own, model), bf16)], (far, got_far), moved=mb)
        parts = [mine, got_near, send(far, lambda group, z: (group, z ^ 2))]
    else:
        parts = [parts[0]] + [send(parts[k], shift_z(-k)) for k in range(1, depth)]

    dout, dact = call(
        back_body,
        [((cells, channels), bf16), ((cells, hid), f32)],
        (wet, ocean_cotangent.reshape(cells, channels), ocean_w_out),
        flops=2 * cells * channels * hid,
        moved=2 * mb,
    )

    line = -(-(tile_y + 2) // 16) * 16
    field, side, row_first, row_last = call(
        functools.partial(field_body, depth, tile_x, tile_y, rows_at),
        [((cells, channels), bf16), ((2 * tile_x, channels), bf16)]
        + [((line, channels), bf16)] * 2,
        (me, state, wet, edges[1], edges[depth - 1], *moved),
        specs=[SMEM] + [VMEM] * (4 + depth),
        moved=mb,
    )
    top = send(row_last, next_group(1))
    low = send(row_first, next_group(-1))

    split = groups == 8
    grad_outs = [((2 * hid, channels), f32)]
    if split:
        grad_outs = [((4, hid // 4, channels), f32), ((4, hid // 4, channels), bf16)]
    outs = call(
        functools.partial(ocean_body, depth, tile_x, tile_y, split),
        [((cells, channels), bf16)] + grad_outs,
        (
            me,
            field,
            side,
            top,
            low,
            wet,
            dout,
            dact,
            conv_kernel,
            ocean_gain,
            ocean_w_in,
            ocean_w_out,
        ),
        specs=[SMEM] + [VMEM] * 11,
        scratch=[pltpu.VMEM((tile_x + 2, tile_y + 16, channels), f32)],
        flops=8 * cells * channels * hid,
        moved=5 * mb,
        tanhs=cells * hid,
    )
    ocean_out = outs[0].reshape(tile_x, tile_y, channels)
    if split:
        keep, give = outs[1:]
        got = send(give, flip(1))
        rows = hid // 4
        plane = call(
            functools.partial(plane_body, depth),
            [((rows, channels), f32)] + [((rows, channels), bf16)] * 3,
            (me, keep, got),
            specs=[SMEM, VMEM, VMEM],
            moved=2 * mb,
        )
        arrived = [send(plane[m], flip(2 * m)) for m in (1, 2, 3)]
        rows = rows // depth
        slabs = call(
            functools.partial(line_body, depth),
            [((rows, channels), f32)] + [((rows, channels), bf16)] * (depth - 1),
            (me, plane[0], *arrived),
            specs=[SMEM] + [VMEM] * 4,
            scratch=[pltpu.VMEM((rows * depth, channels), f32)],
            moved=mb,
        )
        arrived = [send(slabs[k], shift_z(-k)) for k in range(1, depth)]
        (weight_grads,) = call(
            sum_body, [((rows, channels), f32)], (slabs[0], *arrived), moved=mb // 4
        )
    else:
        weight_grads = lax.psum_scatter(outs[1], ALL, scatter_dimension=0, tiled=True)

    (atmos_out,) = call(sum_body, [((own, model), bf16)], (own_rows, *parts), moved=2 * mb)
    return (atmos_out, ocean_out, weight_grads)


def solution(mesh):
    in_specs = (
        P(("grp", "tile"), None),
        P(),
        P(("grp", "tile"), "tp"),
        P(("grp", "tile"), "tp"),
        P(),
        P(ALL, None),
        P(ALL, None, None, None),
        P(("grp", "tile"), "tp", None),
        P(("grp", "tile"), "tp"),
        P(),
        P(),
        P(),
        P(),
        P(("grp", "tile"), "tp", None),
    )
    out_specs = (
        P(ALL, None),
        P(("grp", "tile"), "tp", None),
        P(ALL, None),
    )
    return jax.shard_map(step, mesh=mesh, in_specs=in_specs, out_specs=out_specs, check_vma=False)
```

```python
import functools

import jax
import jax.numpy as jnp
from jax import lax
from jax.experimental import pallas as pl
from jax.experimental.pallas import tpu as pltpu
from jax.sharding import PartitionSpec as P


LEV = 16
ALL = ("grp", "tile", "tp")

epsilon = 1e-06
bf16 = jnp.bfloat16
f32 = jnp.float32
NT = (((1,), (1,)), ((), ()))
TN = (((0,), (0,)), ((), ()))
VMEM = pl.BlockSpec(memory_space=pltpu.VMEM)
SMEM = pl.BlockSpec(memory_space=pltpu.SMEM)


def send(value, target):
    groups = lax.axis_size("grp") * lax.axis_size("tile")
    depth = lax.axis_size("tp")
    pairs = []
    for group in range(groups):
        for z in range(depth):
            to = target(group, z)
            if to is not None:
                pairs.append((group * depth + z, to[0] * depth + to[1]))
    return lax.ppermute(value, ALL, pairs)


def flip(mask):
    return lambda group, z: (group ^ mask, z)


def shift_z(step):
    depth = lax.axis_size("tp")
    return lambda group, z: (group, (z + step) % depth)


def next_group(step):
    groups = lax.axis_size("grp") * lax.axis_size("tile")
    return lambda group, z: (group + step, z) if 0 <= group + step < groups else None


def gather_rows(block, order):
    groups = lax.axis_size("grp") * lax.axis_size("tile")
    rows = block.shape[0]
    if groups != 8 or rows % 64 != 0:
        full = lax.all_gather(block, ("grp", "tile"), axis=0, tiled=True)
        return [(None, full)]
    masks = {"x": 2, "y": 4}
    held = {0: block}
    for axis in "yx":
        held[masks[axis]] = send(block, flip(masks[axis]))
    leg = masks[order[0]]
    held[6] = send(held[leg], flip(6 - leg))
    for mask in (0, 2, 4, 6):
        held[mask + 1] = send(held[mask], flip(1))
    return sorted(held.items())


def call(body, outs, args, specs=None, scratch=(), flops=0, moved=0, tanhs=0, grant=10):
    return pl.pallas_call(
        body,
        out_shape=[jax.ShapeDtypeStruct(*o) for o in outs],
        in_specs=specs or [VMEM] * len(args),
        out_specs=[VMEM] * len(outs),
        scratch_shapes=list(scratch),
        cost_estimate=pl.CostEstimate(
            flops=int(flops), bytes_accessed=int(moved), transcendentals=int(tanhs)
        ),
        compiler_params=pltpu.CompilerParams(vmem_limit_bytes=grant * 2**20),
    )(*args)


def gelu(x):
    inner = 0.7978845608028654 * (x + 0.044715 * (x * x * x))
    return x * (0.5 * (1.0 + jnp.tanh(inner)))


def gelu_both(x):
    root = 0.7978845608028654
    square = x * x
    t = jnp.tanh(root * (x + 0.044715 * (square * x)))
    half = 0.5 * (1.0 + t)
    slope = half + 0.5 * x * (1.0 - t * t) * (root * (1.0 + 3.0 * 0.044715 * square))
    return x * half, slope


def norm_body(depth, id_ref, x_ref, gain_ref, out_ref, own_ref):
    wide = x_ref[...].astype(f32)
    scale = lax.rsqrt(jnp.mean(wide * wide, axis=-1, keepdims=True) + epsilon)
    out_ref[...] = (wide * scale * gain_ref[...].reshape(1, -1)).astype(bf16)
    own = own_ref.shape[0]
    own_ref[...] = x_ref[pl.ds(pl.multiple_of((id_ref[0] % depth) * own, own), own), :]


def edge_columns(flat, tile_x, tile_y):
    grid = flat.reshape(tile_x, tile_y, flat.shape[-1])
    return grid[:, 0], grid[:, tile_y - 1]


def edge_rows(sources, tile_x, halves):
    at_state = -(-sources // 16) * 16
    at_depth = at_state + 2 * halves * tile_x
    return at_state, at_depth, at_depth + 2 * tile_x


def prep_body(index_ref, state_ref, depth_ref, out_ref, wet_ref):
    tile_x, tile_y = depth_ref.shape
    blocks, per_block = index_ref.shape
    inner = out_ref.shape[1]
    channels = state_ref.shape[1]
    halves = channels // inner
    at_state, at_depth, _ = edge_rows(blocks * per_block, tile_x, halves)
    row = lax.broadcasted_iota(jnp.int32, (at_state, inner), 0)
    table = jnp.zeros(row.shape, jnp.int32)
    for b in range(blocks):
        for k in range(per_block):
            table = jnp.where(row == b * per_block + k, index_ref[b, k], table)
    out_ref[:at_state, :] = table.astype(f32).astype(bf16)
    first, last = edge_columns(state_ref[...].astype(f32), tile_x, tile_y)
    edges = [e[:, h * inner : (h + 1) * inner] for e in (last, first) for h in range(halves)]
    out_ref[at_state:at_depth, :] = jnp.concatenate(edges, axis=0).astype(bf16)
    deep = depth_ref[...].astype(f32)
    edges = [
        jnp.broadcast_to(deep[:, at : at + 1], (tile_x, inner)) for at in (tile_y - 1, 0)
    ]
    out_ref[at_depth:, :] = jnp.concatenate(edges, axis=0).astype(bf16)
    level = lax.broadcasted_iota(jnp.int32, (tile_y, channels), 1) // (channels // LEV)
    down = deep.T
    for x in range(tile_x):
        wet = jnp.where(level.astype(f32) < down[:, x : x + 1], 1.0, 0.0)
        wet_ref[x * tile_y : (x + 1) * tile_y, :] = wet.astype(bf16)


def build_matrix(blocks, weight_ref, edge_ref, out_ref):
    sources, rows, inner = weight_ref.shape
    per_block = sources // blocks
    count = out_ref.shape[1] // inner
    for b in range(blocks):
        taken = range(b * per_block, (b + 1) * per_block)
        values = [weight_ref[n].astype(f32) for n in taken]
        picks = [edge_ref[n : n + 1, :].astype(f32) for n in taken]
        for j in range(count):
            total = jnp.zeros((rows, inner), f32)
            for value, pick in zip(values, picks):
                total = total + jnp.where(pick == float(j), 1.0, 0.0) * value
            out_ref[b * rows : (b + 1) * rows, j * inner : (j + 1) * inner] = total.astype(bf16)


def place_blocks(me, pieces, refs, rows, full_ref, paired):
    pairs = sorted({mask // 2 for mask in pieces if mask is not None})
    for mask, ref in zip(pieces, refs):
        if mask is None:
            full_ref[...] = ref[...]
            continue
        start = (me ^ mask) * rows
        if paired:
            start = pairs.index(mask // 2) * 2 * rows + ((me % 2) ^ (mask % 2)) * rows
        full_ref[pl.ds(pl.multiple_of(start, 64), rows), :] = ref[...]


def add_product(me, x_ref, pieces, rows, full_ref, at, step, total):
    if pieces[0] is None:
        part = jnp.dot(x_ref[...], full_ref[:, at : at + step], preferred_element_type=f32)
        return part if total is None else total + part
    for n, pair in enumerate(sorted({mask // 2 for mask in pieces})):
        start = pl.multiple_of(((me // 2) ^ pair) * (2 * rows), 128)
        part = jnp.dot(
            x_ref[:, pl.ds(start, 2 * rows)],
            full_ref[n * 2 * rows : (n + 1) * 2 * rows, at : at + step],
            preferred_element_type=f32,
        )
        total = part if total is None else total + part
    return total


def early_body(pieces, rows, depth, id_ref, x_ref, *refs):
    blocks, (out_ref, full) = refs[:-2], refs[-2:]
    me = id_ref[0] // depth
    place_blocks(me, pieces, blocks, rows, full, True)
    width = out_ref.shape[1]
    step = 256 if width % 256 == 0 else width
    for at in range(0, width, step):
        out_ref[:, at : at + step] = add_product(me, x_ref, pieces, rows, full, at, step, None)


def first_body(
    pieces, rows, depth, tile_x, tile_y, remap, early, id_ref, x_ref, own_ref, both_ref, *refs
):
    mats, tables, refs = refs[:depth], refs[depth : 2 * depth], refs[2 * depth :]
    sums, refs = refs[: int(early)], refs[int(early) :]
    blocks, refs = refs[: len(pieces)], refs[len(pieces) :]
    hid_ref, moved, refs = refs[0], refs[1 : depth + 1], refs[depth + 1 :]
    full, flux, dense = refs[0], refs[1], refs[2:]
    me = id_ref[0] // depth
    z = id_ref[0] % depth
    place_blocks(me, pieces, blocks, rows, full, True)
    for k in range(depth):
        build_matrix(remap, mats[k], tables[k], dense[k])
    width = hid_ref.shape[1]
    step = 256 if width % 256 == 0 else width
    total = jnp.zeros(flux.shape, f32)
    for at in range(0, width, step):
        pre = sums[0][:, at : at + step] if early else None
        pre = add_product(me, x_ref, pieces, rows, full, at, step, pre)
        hidden = gelu(pre).astype(bf16)
        hid_ref[:, at : at + step] = hidden
        total = total + lax.dot_general(
            hidden, both_ref[:, at : at + step], NT, preferred_element_type=f32
        )
    flux[...] = total
    own = own_ref.shape[0]
    mine = pl.ds(pl.multiple_of(z * own, own), own)
    flux[mine, :] += own_ref[...]
    low = flux[...].astype(bf16)
    cells = tile_x * tile_y
    results = [jnp.dot(m[...], low, preferred_element_type=f32) for m in dense]
    edges = [edge_columns(r, tile_x, tile_y) for r in results]
    for k in range(depth):
        moved[k][:cells, :] = results[k].astype(bf16)
        sides = [edges[(k + 1) % depth][1], edges[(k - 1) % depth][0]]
        moved[k][cells:, :] = jnp.concatenate(sides, axis=0).astype(bf16)


def both_body(pieces, rows, depth, id_ref, proj_ref, own_ref, *refs):
    blocks, (out_ref, flux_ref, full) = refs[:-3], refs[-3:]
    place_blocks(id_ref[0] // depth, pieces, blocks, rows, full, False)
    out_ref[...] = lax.dot_general(
        proj_ref[...], full[...], TN, preferred_element_type=f32
    ).astype(bf16)
    flux_ref[...] = jnp.dot(own_ref[...], proj_ref[...], preferred_element_type=f32)


def back_body(wet_ref, cot_ref, wout_ref, dout_ref, dact_ref):
    dout = (cot_ref[...].astype(f32) * wet_ref[...].astype(f32)).astype(bf16)
    dout_ref[...] = dout
    step = dact_ref.shape[1] // 4
    for at in range(0, dact_ref.shape[1], step):
        dact_ref[:, at : at + step] = lax.dot_general(
            dout, wout_ref[at : at + step, :], NT, preferred_element_type=f32
        )


def second_body(pieces, rows, depth, shards, id_ref, hid_ref, *refs):
    blocks, refs = refs[: len(pieces)], refs[len(pieces) :]
    parts, (full, sums) = refs[:-2], refs[-2:]
    z = id_ref[0] % depth
    place_blocks(id_ref[0] // depth, pieces, blocks, rows, full, False)
    tokens, width = sums.shape
    own = tokens // depth
    step = 256 if width % 256 == 0 else width
    for at in range(0, width, step):
        sums[:, at : at + step] = lax.dot_general(
            hid_ref[...], full[at : at + step, :], NT, preferred_element_type=f32
        ).astype(bf16)
    for ref, rule in zip(parts, shards):
        for n, of in enumerate(rule):
            start = pl.multiple_of(of(z) * own, own)
            ref[n * own : (n + 1) * own, :] = sums[pl.ds(start, own), :]


def field_body(depth, tile_x, tile_y, rows_at, id_ref, state_ref, wet_ref, west_ref, east_ref, *refs):
    parts, refs = refs[:depth], refs[depth:]
    field_ref, side_ref, first_ref, last_ref = refs
    z = id_ref[0] % depth
    cells = tile_x * tile_y
    channels = state_ref.shape[1]
    total = parts[0][...].astype(f32)
    for p in parts[1:]:
        total = total + p[...].astype(f32)
    total = total.astype(bf16).astype(f32)
    field = ((state_ref[...].astype(f32) + total[:cells]) * wet_ref[...].astype(f32)).astype(bf16)
    field_ref[...] = field
    at_state, at_depth, _ = rows_at
    inner = west_ref.shape[1]
    halves = channels // inner
    level = lax.broadcasted_iota(jnp.int32, (tile_x, channels), 1) // (channels // LEV)
    sides = []
    for which, ref, inside in ((0, west_ref, z > 0), (1, east_ref, z < depth - 1)):
        at = at_state + which * halves * tile_x
        state = jnp.concatenate(
            [ref[at + h * tile_x : at + (h + 1) * tile_x, :].astype(f32) for h in range(halves)],
            axis=1,
        )
        at = at_depth + which * tile_x
        deep = jnp.concatenate([ref[at : at + tile_x, :].astype(f32)] * halves, axis=1)
        deep = deep * jnp.where(inside, 1.0, 0.0).astype(f32)
        at = cells + which * tile_x
        sides.append(jnp.where(level.astype(f32) < deep, state + total[at : at + tile_x], 0.0))
    side_w, side_e = sides
    side_ref[...] = jnp.concatenate([side_w, side_e], axis=0).astype(bf16)
    spare = jnp.zeros((first_ref.shape[0] - tile_y - 2, channels), f32)
    wide = field.astype(f32)
    for ref, row in ((first_ref, 0), (last_ref, tile_x - 1)):
        ref[...] = jnp.concatenate(
            [
                wide[row * tile_y : (row + 1) * tile_y],
                side_w[row : row + 1],
                side_e[row : row + 1],
                spare,
            ],
            axis=0,
        ).astype(bf16)


def ocean_body(
    depth, tile_x, tile_y, split, id_ref, field_ref, side_ref, top_ref, low_ref, wet_ref, dout_ref, dact_ref,
    kern_ref, gain_ref, win_ref, wout_ref, *refs
):
    out_ref, refs = refs[0], refs[1:]
    pad, sums = refs[-2:]
    cells, channels = field_ref.shape
    core = (id_ref[0] // depth) % 2
    at = 8
    pad[1 : tile_x + 1, at : at + tile_y, :] = (
        field_ref[...].astype(f32).reshape(tile_x, tile_y, channels)
    )
    side = side_ref[...].astype(f32)
    pad[1 : tile_x + 1, at - 1, :] = side[:tile_x]
    pad[1 : tile_x + 1, at + tile_y, :] = side[tile_x:]
    for row, ref in ((0, top_ref), (tile_x + 1, low_ref)):
        line = ref[...].astype(f32)
        pad[row, at : at + tile_y, :] = line[:tile_y]
        pad[row, at - 1 : at, :] = line[tile_y : tile_y + 1]
        pad[row, at + tile_y : at + tile_y + 1, :] = line[tile_y + 1 : tile_y + 2]
    conv = jnp.zeros((tile_x, tile_y, channels), f32)
    for i in range(3):
        for j in range(3):
            tap = kern_ref[i, j].reshape(1, 1, channels)
            conv = conv + tap * pad[i : i + tile_x, at - 1 + j : at - 1 + j + tile_y, :]
    conv = conv.reshape(cells, channels)
    centred = conv - jnp.mean(conv, axis=-1, keepdims=True)
    variance = jnp.mean(centred * centred, axis=-1, keepdims=True)
    normed = (centred * lax.rsqrt(variance + epsilon) * gain_ref[...].reshape(1, -1)).astype(bf16)
    wet = wet_ref[...].astype(f32)
    dout = dout_ref[...]
    hid = win_ref.shape[1]
    step = hid // 4
    total = jnp.zeros((cells, channels), f32)
    for c in range(4):
        span = slice(c * step, (c + 1) * step)
        pre = jnp.dot(normed, win_ref[:, span], preferred_element_type=f32)
        value, slope = gelu_both(pre)
        act = value.astype(bf16)
        total = total + jnp.dot(act, wout_ref[span, :], preferred_element_type=f32)
        dpre = (dact_ref[:, span] * slope).astype(bf16)
        grads = (
            lax.dot_general(dpre, normed, TN, preferred_element_type=f32),
            lax.dot_general(act, dout, TN, preferred_element_type=f32),
        )
        for which, grad in enumerate(grads):
            (sums if split else refs[0])[which * hid + c * step : which * hid + (c + 1) * step, :] = grad
    if split:
        for spot in range(4):
            for ref, which in ((refs[0], core), (refs[1], 1 - core)):
                start = pl.multiple_of((2 * spot + which) * step, step)
                ref[spot] = sums[pl.ds(start, step), :].astype(ref.dtype)
    out_ref[...] = ((field_ref[...].astype(f32) + total) * wet).astype(bf16)


def plane_body(depth, id_ref, keep_ref, got_ref, own_ref, *outs):
    place = id_ref[0] // depth // 2
    for mask, ref in enumerate((own_ref,) + outs):
        spot = place ^ mask
        ref[...] = (keep_ref[spot] + got_ref[spot].astype(f32)).astype(ref.dtype)


def line_body(depth, id_ref, own_ref, a_ref, b_ref, c_ref, *refs):
    outs, total = refs[:-1], refs[-1]
    z = id_ref[0] % depth
    arrived = a_ref[...].astype(f32) + b_ref[...].astype(f32) + c_ref[...].astype(f32)
    total[...] = own_ref[...] + arrived
    rows = total.shape[0] // depth
    for k, ref in enumerate(outs):
        start = pl.multiple_of(((z - k + depth) % depth) * rows, rows)
        ref[...] = total[pl.ds(start, rows), :].astype(ref.dtype)


def sum_body(*refs):
    out_ref = refs[-1]
    total = refs[0][...].astype(f32)
    for ref in refs[1:-1]:
        total = total + ref[...].astype(f32)
    out_ref[...] = total.astype(out_ref.dtype)


def step(
    atmos_state,
    atmos_gain,
    w_first,
    w_second,
    flux_proj,
    remap_index,
    remap_weight,
    ocean_state,
    depth_levels,
    conv_kernel,
    ocean_gain,
    ocean_w_in,
    ocean_w_out,
    ocean_cotangent,
):
    depth = lax.axis_size("tp")
    groups = lax.axis_size("grp") * lax.axis_size("tile")
    me = lax.axis_index(ALL).astype(jnp.int32).reshape(1)
    tokens, model = atmos_state.shape
    own = tokens // depth
    channels = flux_proj.shape[1]
    share = w_first.shape[1]
    tile_x, tile_y, _ = ocean_state.shape
    cells = tile_x * tile_y
    hid = ocean_w_in.shape[1]
    mb = 2**20

    second = gather_rows(w_second, "yx")
    first = gather_rows(w_first, "xy")
    state = ocean_state.reshape(cells, channels)
    blocks, per_block, block_rows, inner = remap_weight.shape
    rows_at = edge_rows(blocks * per_block, tile_x, channels // inner)
    weights = remap_weight.reshape(blocks * per_block, block_rows, inner)
    steps = range(1, depth)
    mats = [weights] + [send(weights, shift_z(k)) for k in steps]
    edge, wet = call(
        prep_body,
        [((rows_at[2], inner), bf16), ((cells, channels), bf16)],
        (remap_index, state, depth_levels),
        specs=[SMEM, VMEM, VMEM],
        moved=mb,
    )
    edges = [edge] + [send(edge, shift_z(k)) for k in steps]
    normed, own_rows = call(
        functools.partial(norm_body, depth),
        [((tokens, model), bf16), ((own, model), bf16)],
        (me, atmos_state, atmos_gain),
        specs=[SMEM, VMEM, VMEM],
        moved=4 * mb,
    )

    rows = w_second.shape[0]
    second_at = [p[0] for p in second]
    second = [p[1] for p in second]
    both, own_flux = call(
        functools.partial(both_body, second_at, rows, depth),
        [((channels, share), bf16), ((own, channels), f32)],
        (me, flux_proj, own_rows, *second),
        specs=[SMEM, VMEM, VMEM] + [VMEM] * len(second),
        scratch=[pltpu.VMEM((model, share), bf16)],
        flops=2 * model * share * channels,
        moved=3 * mb,
    )

    rows = w_first.shape[0]
    early = first[0][0] is not None
    sums = []
    if early:
        soon = [p for p in first if p[0] < 6]
        first = [p for p in first if p[0] >= 6]
        sums = call(
            functools.partial(early_body, [p[0] for p in soon], rows, depth),
            [((tokens, share), f32)],
            (me, normed, *[p[1] for p in soon]),
            specs=[SMEM, VMEM] + [VMEM] * len(soon),
            scratch=[pltpu.VMEM((6 * rows, share), bf16)],
            flops=2 * tokens * share * 6 * rows,
            moved=5 * mb,
        )
    outs = call(
        functools.partial(
            first_body,
            [p[0] for p in first],
            rows,
            depth,
            tile_x,
            tile_y,
            blocks,
            early,
        ),
        [((tokens, share), bf16)] + [((cells + 2 * tile_x, channels), bf16)] * depth,
        (me, normed, own_flux, both, *mats, *edges, *sums, *[p[1] for p in first]),
        specs=[SMEM] + [VMEM] * (3 + 2 * depth + len(sums)) + [VMEM] * len(first),
        scratch=[
            pltpu.VMEM((2 * rows if early else model, share), bf16),
            pltpu.VMEM((tokens, channels), f32),
        ]
        + [pltpu.VMEM((cells, tokens), bf16)] * depth,
        flops=2 * tokens * share * (2 * rows + channels),
        moved=5 * mb,
        tanhs=tokens * share,
    )
    hidden, moved = outs[0], outs[1:]
    moved = [moved[0]] + [send(moved[k], shift_z(-k)) for k in range(1, depth)]

    rows = w_second.shape[0]
    pairwise = depth == 4
    if pairwise:
        shards = [
            [lambda z: z],
            [lambda z: z ^ 2],
            [lambda z: z ^ 3],
            [lambda z: z ^ 1],
        ]
    else:
        shards = [[lambda z, k=k: (z - k + depth) % depth] for k in range(depth)]
    parts = call(
        functools.partial(second_body, second_at, rows, depth, shards),
        [((own * len(rule), model), bf16) for rule in shards],
        (me, hidden, *second),
        specs=[SMEM, VMEM] + [VMEM] * len(second),
        scratch=[
            pltpu.VMEM((model, share), bf16),
            pltpu.VMEM((tokens, model), bf16),
        ],
        flops=2 * tokens * model * share,
        moved=6 * mb,
    )
    if pairwise:
        mine, far, give_far, give_near = parts
        near_z = lambda group, z: (group, z ^ 1)
        got_far = send(give_far, near_z)
        got_near = send(give_near, near_z)
        (far,) = call(sum_body, [((own, model), bf16)], (far, got_far), moved=mb)
        parts = [mine, got_near, send(far, lambda group, z: (group, z ^ 2))]
    else:
        parts = [parts[0]] + [send(parts[k], shift_z(-k)) for k in range(1, depth)]

    dout, dact = call(
        back_body,
        [((cells, channels), bf16), ((cells, hid), f32)],
        (wet, ocean_cotangent.reshape(cells, channels), ocean_w_out),
        flops=2 * cells * channels * hid,
        moved=2 * mb,
    )

    line = -(-(tile_y + 2) // 16) * 16
    field, side, row_first, row_last = call(
        functools.partial(field_body, depth, tile_x, tile_y, rows_at),
        [((cells, channels), bf16), ((2 * tile_x, channels), bf16)]
        + [((line, channels), bf16)] * 2,
        (me, state, wet, edges[1], edges[depth - 1], *moved),
        specs=[SMEM] + [VMEM] * (4 + depth),
        moved=mb,
    )
    top = send(row_last, next_group(1))
    low = send(row_first, next_group(-1))

    split = groups == 8
    grad_outs = [((2 * hid, channels), f32)]
    if split:
        grad_outs = [((4, hid // 4, channels), f32), ((4, hid // 4, channels), bf16)]
    outs = call(
        functools.partial(ocean_body, depth, tile_x, tile_y, split),
        [((cells, channels), bf16)] + grad_outs,
        (
            me,
            field,
            side,
            top,
            low,
            wet,
            dout,
            dact,
            conv_kernel,
            ocean_gain,
            ocean_w_in,
            ocean_w_out,
        ),
        specs=[SMEM] + [VMEM] * 11,
        scratch=[
            pltpu.VMEM((tile_x + 2, tile_y + 16, channels), f32),
            pltpu.VMEM((2 * hid, channels), f32),
        ],
        flops=8 * cells * channels * hid,
        moved=5 * mb,
        tanhs=cells * hid,
    )
    ocean_out = outs[0].reshape(tile_x, tile_y, channels)
    if split:
        keep, give = outs[1:]
        got = send(give, flip(1))
        rows = hid // 4
        plane = call(
            functools.partial(plane_body, depth),
            [((rows, channels), f32)] + [((rows, channels), bf16)] * 3,
            (me, keep, got),
            specs=[SMEM, VMEM, VMEM],
            moved=2 * mb,
        )
        arrived = [send(plane[m], flip(2 * m)) for m in (1, 2, 3)]
        rows = rows // depth
        slabs = call(
            functools.partial(line_body, depth),
            [((rows, channels), f32)] + [((rows, channels), bf16)] * (depth - 1),
            (me, plane[0], *arrived),
            specs=[SMEM] + [VMEM] * 4,
            scratch=[pltpu.VMEM((rows * depth, channels), f32)],
            moved=mb,
        )
        arrived = [send(slabs[k], shift_z(-k)) for k in range(1, depth)]
        (weight_grads,) = call(
            sum_body, [((rows, channels), f32)], (slabs[0], *arrived), moved=mb // 4
        )
    else:
        weight_grads = lax.psum_scatter(outs[1], ALL, scatter_dimension=0, tiled=True)

    (atmos_out,) = call(sum_body, [((own, model), bf16)], (own_rows, *parts), moved=2 * mb)
    return (atmos_out, ocean_out, weight_grads)


def solution(mesh):
    in_specs = (
        P(("grp", "tile"), None),
        P(),
        P(("grp", "tile"), "tp"),
        P(("grp", "tile"), "tp"),
        P(),
        P(ALL, None),
        P(ALL, None, None, None),
        P(("grp", "tile"), "tp", None),
        P(("grp", "tile"), "tp"),
        P(),
        P(),
        P(),
        P(),
        P(("grp", "tile"), "tp", None),
    )
    out_specs = (
        P(ALL, None),
        P(("grp", "tile"), "tp", None),
        P(ALL, None),
    )
    return jax.shard_map(step, mesh=mesh, in_specs=in_specs, out_specs=out_specs, check_vma=False)
```
